1024 devices in a mesh: ctx: 16 (over y, x), exp: 64 (over z, core).
Axes of the slice: x: 4, y: 4, z: 32, core: 2. Of those that a mesh axis runs over, the one named last changes fastest.
Arguments:
- tokens: bfloat16 [8192, 4096], P('exp', 'ctx'), may hold values from -6 to 6
- cotangent: bfloat16 [8192, 4096], P('exp', 'ctx'), may hold values from -6 to 6
- routes: int32 [8192, 8], P('exp'), may hold values from 0 to 127, all different within a row; in each aligned block of 128 rows (0 to 127, 128 to 255, ...) at most 12 rows name the same one
- router_weight: float32 [4096, 128], P('ctx'), may hold values from -0.09375 to 0.09375
- expert_out: bfloat16 [128, 768, 4096], P('exp', None, 'ctx'), may hold values from -6 to 6
Outputs:
- mixed: bfloat16 [8192, 4096], P('exp', 'ctx')
- token_grad: bfloat16 [8192, 4096], P('exp', 'ctx')
- router_grad: float32 [4096, 128], P('ctx')
- slot_grad: bfloat16 [128, 768, 4096], P('exp', None, 'ctx')
The draws below stay inside these ranges and needn't reach their ends.
Inputs may be any that keep to these rules, and one draw needn't show every extreme that they name: `routes`: each row names 8 different experts; among the rows of one index of exp no expert is named more than 12 times.
All inputs are finite; a program needn't handle non-finite values.
Results may differ from the reference program's by a relative error of at most 0.00105.
Values may be sent and summed in bfloat16 or wider, within the bound.
No kernel may reach another device: no remote copies, remote signals or barrier semaphores. Data moves between devices by JAX's collectives and lax.ppermute only.
A program may use at most 32 MiB of HBM per device.

```python
import math
import jax
import jax.numpy as jnp
import numpy as np
from jax import lax

D = 4096
TOP = 8
TOK_DEV = 128
EXPERTS = 128
CAP = 12
TOKENS = 8192
N_EXP = 64


def block_scale(stream_key, shape, split, low, high):
    def one(dim, shards_of):
        draws = jax.random.uniform(jax.random.fold_in(jax.random.fold_in(stream_key, 6), dim), (shards_of,), jnp.float32, low / len(split), high / len(split))
        return jnp.repeat(jnp.exp(draws), shape[dim] // shards_of).reshape((-1,) + (1,) * (len(shape) - dim - 1))

    factor_of = one(*split[0])
    for cut in split[1:]:
        factor_of = factor_of * one(*cut)
    return factor_of


def deal_out(stream_key, own, number, rows, count, top, limit, slope):
    sequence = jax.random.permutation(stream_key, count)
    heavy_load, usual = portions_of(count, rows * top, limit, slope, True), portions_of(count, rows * top, limit, slope, False)
    places = jnp.arange(count)

    def named(tallies, turn):
        used = int((tallies > 0).sum())
        fixed = max(1, used // 4)
        passed = fixed + (places - fixed + turn * (used - fixed)) % max(1, count - fixed)
        return jnp.zeros((count,), jnp.int32).at[sequence[jnp.where(places < fixed, places, passed)]].set(jnp.asarray(tallies, jnp.int32))

    tallies = jnp.where(number % 4 == 0, named(heavy_load, number // 4), named(usual, number - number // 4 - 1))
    mixed = jax.random.permutation(jax.random.fold_in(own, 3), count)
    source_of, receiver = mixed[0:count // 2 * 2:2], mixed[1:count // 2 * 2:2]
    margin = jnp.minimum(tallies[source_of] - 1, limit - tallies[receiver]) // 2
    margin = jnp.where((source_of == sequence[0]) | (receiver == sequence[0]) | (tallies[receiver] == 0), 0, jnp.maximum(margin, 0))
    passed = jax.random.randint(jax.random.fold_in(own, 4), (count // 2,), 0, 1 << 20) % (margin + 1)
    tallies = tallies.at[source_of].add(-passed).at[receiver].add(passed)
    members = jnp.searchsorted(jnp.cumsum(tallies), jnp.arange(rows * top), side="right").astype(jnp.int32)
    listing = members.reshape(top, rows).T
    listing = listing[jax.random.permutation(jax.random.fold_in(own, 1), rows)]
    turn = jax.random.randint(jax.random.fold_in(own, 2), (rows, 1), 0, top)
    return jnp.take_along_axis(listing, (jnp.arange(top)[None, :] + turn) % top, axis=1)


def portions_of(count, total, most, lean, full):
    portions = [(1 << 20) // math.isqrt(rank ** lean) + 1 for rank in range(1, count + 1)]
    largest = most if full else min(most, max(-(-total // count), total * portions[0] // sum(portions)))
    least = 1 if total - largest >= count - 1 else 0
    holding, surplus = [largest] + [least] * (count - 1), total - largest - least * (count - 1)
    while surplus > 0:
        free = [i for i in range(1, count) if holding[i] < largest] or [i for i in range(1, count) if holding[i] < most]
        whole, remaining = sum([portions[i] for i in free]), surplus
        for i in free:
            more = min(most - holding[i], max(1, remaining * portions[i] // whole), surplus)
            holding[i] = holding[i] + more
            surplus = surplus - more
    return np.array(holding)


def scatter_about(rng, extent, scale, most, split=(), kind=jnp.bfloat16):
    drawn = jax.random.normal(rng, extent, jnp.float32) * scale
    if len(split) > 0:
        drawn = block_scale(rng, extent, split, -0.22, 0.18) * drawn
    return jnp.clip(drawn, min=-most, max=most).astype(kind)


def setup_inputs(seed: int = 0) -> dict:
    seeds = jax.random.split(jax.random.key(seed), 6)
    tokens = scatter_about(seeds[0], (TOKENS, D), 1.0, 6.0, ((0, 64), (1, 16)))
    cotangent = scatter_about(seeds[1], (TOKENS, D), 1.0, 6.0, ((0, 64), (1, 16)))
    routes_keys = jax.random.split(jax.random.fold_in(seeds[2], 1), TOKENS // TOK_DEV)
    routes_turns = jax.random.permutation(jax.random.fold_in(seeds[2], 3), TOKENS // TOK_DEV)
    routes = jax.vmap(lambda own, number: deal_out(jax.random.fold_in(seeds[2], 2), own, number, TOK_DEV, EXPERTS, TOP, CAP, 2))(routes_keys, routes_turns).reshape((TOKENS, TOP))
    router_weight = scatter_about(seeds[3], (D, EXPERTS), D ** -0.5, 0.09375, ((0, 16),), jnp.float32)
    expert_out = scatter_about(seeds[4], (EXPERTS, N_EXP * CAP, D), 1.0, 6.0, ((0, 64), (2, 16)))
    return {"tokens": tokens, "cotangent": cotangent, "routes": routes, "router_weight": router_weight, "expert_out": expert_out}


def slot_rows(routes):
    blocks = routes.reshape(N_EXP, TOK_DEV * TOP)
    onehot = (blocks[:, :, None] == jnp.arange(EXPERTS, dtype=jnp.int32)[None, None, :]).astype(jnp.int32)
    earlier = jnp.cumsum(onehot, axis=1) - onehot
    position = jnp.sum(earlier * onehot, axis=2).astype(jnp.int32)
    offsets = (jnp.arange(N_EXP, dtype=jnp.int32) * CAP)[:, None]
    return (offsets + position).reshape(TOKENS, TOP).astype(jnp.int32)


def reference(tokens, cotangent, routes, router_weight, expert_out):
    slot_row = slot_rows(routes)
    highest = lax.Precision.HIGHEST
    logits = jnp.dot(tokens.astype(jnp.float32), router_weight, precision=highest)
    expo = jnp.exp(logits)
    probs = expo / jnp.sum(expo, axis=1, keepdims=True)
    chosen = jnp.take_along_axis(probs, routes, axis=1)
    total = jnp.sum(chosen, axis=1, keepdims=True)
    gates = chosen / total

    def block(inputs):
        cot, chosen_routes, chosen_rows, weights = inputs
        pairs = expert_out[chosen_routes, chosen_rows].astype(jnp.float32)
        mixed_block = jnp.sum(weights[:, :, None] * pairs, axis=1).astype(jnp.bfloat16)
        dot_block = jnp.sum(cot.astype(jnp.float32)[:, None, :] * pairs, axis=2)
        return mixed_block, dot_block

    mixed, dots = lax.map(block, (cotangent.reshape(N_EXP, TOK_DEV, D), routes.reshape(N_EXP, TOK_DEV, TOP),
                                  slot_row.reshape(N_EXP, TOK_DEV, TOP), gates.reshape(N_EXP, TOK_DEV, TOP)))
    mixed = mixed.reshape(TOKENS, D)
    dots = dots.reshape(TOKENS, TOP)
    weighted = (gates[:, :, None] * cotangent.astype(jnp.float32)[:, None, :]).astype(jnp.bfloat16)
    slot_grad = jnp.zeros((EXPERTS, N_EXP * CAP, D), jnp.bfloat16).at[routes, slot_row].set(weighted)
    dchosen = (dots - jnp.sum(dots * gates, axis=1, keepdims=True)) / total
    match = (routes[:, :, None] == jnp.arange(EXPERTS, dtype=jnp.int32)[None, None, :]).astype(jnp.float32)
    spread = jnp.sum(match * dchosen[:, :, None], axis=1)
    dlogits = probs * (spread - jnp.sum(chosen * dchosen, axis=1, keepdims=True))
    token_grad = jnp.dot(dlogits, router_weight.T, precision=highest).astype(jnp.bfloat16)
    router_grad = jnp.dot(tokens.astype(jnp.float32).T, dlogits, precision=highest)
    return mixed, token_grad, router_grad, slot_grad
```

```python
import functools

import jax
import jax.numpy as jnp
from jax import lax
from jax.experimental import pallas as pl
from jax.experimental.pallas import tpu as pltpu
from jax.sharding import Mesh
from jax.sharding import PartitionSpec as P


CTX = ("ctx_0", "ctx_1")
NEAR = ("z_lo", "core")
EXP = ("z_hi", "z_lo", "core")
F32 = jnp.float32
BF16 = jnp.bfloat16
INTERPRET = False
NT = (((1,), (1,)), ((), ()))
HIGHEST = lax.Precision.HIGHEST


def broadcast_exchange(array, axes):
    size = lax.axis_size(axes)
    return lax.all_to_all(
        jnp.broadcast_to(array[None], (size, *array.shape)), axes, 0, 0, tiled=True
    )


def ring_parts(array, axis):
    size = lax.axis_size(axis)
    parts = [array]
    for shift in range(1, size):
        parts.append(lax.ppermute(array, axis, [(i, (i + shift) % size) for i in range(size)]))
    return parts


def ring_sum(array, axis):
    parts = ring_parts(array, axis)
    total = parts[0]
    for part in parts[1:]:
        total = total + part
    return total


def split3(x):
    hi = x.astype(BF16)
    rest = x - hi.astype(F32)
    mid = rest.astype(BF16)
    lo = (rest - mid.astype(F32)).astype(BF16)
    return hi, mid, lo


def call(kernel, outs, *args):
    return pl.pallas_call(
        kernel,
        out_shape=[jax.ShapeDtypeStruct(shape, dtype) for shape, dtype in outs],
        interpret=INTERPRET,
    )(*args)


def gate_kernel(logits_ref, routes_ref, cot_ref, probs_ref, small_ref, code_ref, code_t_ref, wt_ref, pay_ref):
    logits = logits_ref[...]
    experts, tokens = logits.shape
    top = routes_ref.shape[0]
    expo = jnp.exp(logits)
    probs = expo / jnp.sum(expo, axis=0, keepdims=True)
    probs_ref[...] = probs
    which = lax.broadcasted_iota(jnp.int32, (experts, tokens), 0)
    hits = [which == routes_ref[k : k + 1, :] for k in range(top)]
    chosen = jnp.concatenate(
        [jnp.sum(jnp.where(hit, probs, 0.0), axis=0, keepdims=True) for hit in hits], axis=0
    )
    total = jnp.sum(chosen, axis=0, keepdims=True)
    gates = chosen / total
    small_ref[0:top, :] = chosen
    small_ref[top : 2 * top, :] = gates
    small_ref[2 * top : 3 * top, :] = jnp.broadcast_to(total, (top, tokens))
    dense = jnp.zeros((experts, tokens), F32)
    member = jnp.zeros((experts, tokens), F32)
    for k in range(top):
        dense = dense + jnp.where(hits[k], gates[k : k + 1, :], 0.0)
        member = member + jnp.where(hits[k], 1.0, 0.0)
    before = lax.broadcasted_iota(jnp.int32, (tokens, tokens), 0)
    after = lax.broadcasted_iota(jnp.int32, (tokens, tokens), 1)
    upper = jnp.where(before < after, 1.0, 0.0).astype(BF16)
    position = jnp.dot(member.astype(BF16), upper, preferred_element_type=F32)
    code = jnp.where(member > 0.5, position, -1.0)
    code_ref[...] = code
    code_t_ref[...] = code.T
    dense_t = dense.T
    for i, term in enumerate(split3(dense_t)):
        wt_ref[i] = term
    pay_ref[0:tokens, :] = cot_ref[...]
    hi, mid, lo = split3(gates)
    names = routes_ref[...].astype(F32)
    extra = jnp.concatenate(
        [
            jnp.concatenate([names, hi.astype(F32)], axis=1),
            jnp.concatenate([mid.astype(F32), lo.astype(F32)], axis=1),
        ],
        axis=0,
    )
    pay_ref[tokens : tokens + 2 * top, :] = extra.astype(BF16)


def combine_kernel(rows_ref, cot_ref, routes_ref, code_ref, code_t_ref, wt_ref, mixed_ref, dots_ref):
    capacity, experts, width = rows_ref.shape
    cot = cot_ref[...]
    code = code_ref[...]
    code_t = code_t_ref[...]
    top, tokens = routes_ref.shape
    dense = jnp.zeros((experts, tokens), F32)
    mixed = jnp.zeros((tokens, width), F32)
    for s in range(capacity):
        rows = rows_ref[s]
        each = lax.dot_general(rows, cot, NT, preferred_element_type=F32)
        dense = dense + jnp.where(code == float(s), each, 0.0)
        here = code_t == float(s)
        for i in range(3):
            weight = jnp.where(here, wt_ref[i].astype(F32), 0.0).astype(BF16)
            mixed = mixed + jnp.dot(weight, rows, preferred_element_type=F32)
    mixed_ref[...] = mixed.astype(BF16)
    which = lax.broadcasted_iota(jnp.int32, (experts, tokens), 0)
    for k in range(top):
        hit = which == routes_ref[k : k + 1, :]
        dots_ref[k : k + 1, :] = jnp.sum(jnp.where(hit, dense, 0.0), axis=0, keepdims=True)


def router_kernel(parts_ref, routes_ref, small_ref, probs_ref, tok_t_ref, part_ref, dlog_ref):
    dots = parts_ref[0]
    for i in range(1, parts_ref.shape[0]):
        dots = dots + parts_ref[i]
    top, _ = dots.shape
    chosen = small_ref[0:top, :]
    gates = small_ref[top : 2 * top, :]
    total = small_ref[2 * top : 3 * top, :]
    dchosen = (dots - jnp.sum(dots * gates, axis=0, keepdims=True)) / total
    level = jnp.sum(chosen * dchosen, axis=0, keepdims=True)
    probs = probs_ref[...]
    which = lax.broadcasted_iota(jnp.int32, probs.shape, 0)
    spread = jnp.zeros(probs.shape, F32)
    for k in range(top):
        spread = spread + jnp.where(which == routes_ref[k : k + 1, :], dchosen[k : k + 1, :], 0.0)
    dlog = probs * (spread - level)
    tok_t = tok_t_ref[...]
    acc = None
    for term in split3(dlog):
        one = lax.dot_general(tok_t, term, NT, preferred_element_type=F32)
        acc = one if acc is None else acc + one
    part_ref[...] = acc
    dlog_ref[...] = dlog


def token_grad_kernel(dlog_ref, weight_ref, out_ref):
    out_ref[...] = lax.dot_general(
        dlog_ref[...].T, weight_ref[...], NT, precision=HIGHEST, preferred_element_type=F32
    ).astype(BF16)


def owner_kernel(group, capacity, local, first_ref, all_ref, out_ref):
    tokens = 128
    top = 8
    height = tokens + 2 * top
    rows = group * capacity
    first = first_ref[0]
    members, weights = [], []
    for q in range(group):
        extra = all_ref[q * height + tokens : (q + 1) * height, :].astype(F32)
        names = extra[0:top, 0:tokens]
        gates = (extra[0:top, tokens:] + extra[top:, 0:tokens]) + extra[top:, tokens:]
        for e in range(local):
            hit = names == (first + e).astype(F32)
            members.append(jnp.sum(jnp.where(hit, 1.0, 0.0), axis=0, keepdims=True))
            weights.append(jnp.sum(jnp.where(hit, gates, 0.0), axis=0, keepdims=True))
    before = lax.broadcasted_iota(jnp.int32, (tokens, tokens), 0)
    after = lax.broadcasted_iota(jnp.int32, (tokens, tokens), 1)
    upper = jnp.where(before < after, 1.0, 0.0).astype(BF16)
    member = jnp.concatenate(members, axis=0)
    position = jnp.dot(member.astype(BF16), upper, preferred_element_type=F32)
    code = jnp.where(member > 0.5, position, -1000.0)
    row = lax.broadcasted_iota(jnp.int32, (rows, tokens), 0).astype(F32)
    picked = jnp.zeros((local * rows, all_ref.shape[1]), F32)
    weight = [jnp.zeros((rows, tokens), F32) for _ in range(local)]
    for q in range(group):
        picks = []
        for e in range(local):
            n = q * local + e
            pick = (code[n : n + 1, :] + float(q * capacity)) == row
            weight[e] = weight[e] + jnp.where(pick, weights[n], 0.0)
            picks.append(jnp.where(pick, 1.0, 0.0))
        select = jnp.concatenate(picks, axis=0).astype(BF16)
        cot = all_ref[q * height : q * height + tokens, :]
        picked = picked + jnp.dot(select, cot, preferred_element_type=F32)
    for e in range(local):
        gate = jnp.sum(weight[e], axis=1, keepdims=True)
        out_ref[e] = (gate * picked[e * rows : (e + 1) * rows, :]).astype(BF16)


def owner_rows(everyone, first, sources, capacity, local):
    group = min(4, sources)
    height = everyone.shape[0] // sources
    width = everyone.shape[1]
    return pl.pallas_call(
        functools.partial(owner_kernel, group, capacity, local),
        grid_spec=pltpu.PrefetchScalarGridSpec(
            num_scalar_prefetch=1,
            grid=(sources // group,),
            in_specs=[pl.BlockSpec((group * height, width), lambda i, first: (i, 0))],
            out_specs=pl.BlockSpec((local, group * capacity, width), lambda i, first: (0, i, 0)),
        ),
        out_shape=jax.ShapeDtypeStruct((local, sources * capacity, width), BF16),
        interpret=INTERPRET,
    )(first, everyone)


def step(tokens, cotangent, routes, router_weight, expert_out):
    rows, top = routes.shape
    local = expert_out.shape[0]
    sources = lax.axis_size(EXP)
    experts = local * sources
    capacity = expert_out.shape[1] // sources
    width = tokens.shape[1]
    routes_t = routes.T

    sent = expert_out.reshape(local, sources, capacity, width).transpose(1, 2, 0, 3)
    returned = lax.all_to_all(sent, EXP, 0, 0, tiled=True)

    partial_logits = lax.dot_general(
        router_weight, tokens.astype(F32), (((0,), (1,)), ((), ())), precision=HIGHEST
    )
    logits = ring_sum(partial_logits, CTX[1])
    logits = ring_sum(logits, CTX[0])
    square = (experts, rows)
    probs, small, code, code_t, wt, payload = call(
        gate_kernel,
        [
            (square, F32),
            ((3 * top, rows), F32),
            (square, F32),
            ((rows, experts), F32),
            ((3, rows, experts), BF16),
            ((rows + 2 * top, width), BF16),
        ],
        logits, routes_t, cotangent,
    )
    everyone = lax.all_gather(payload, EXP, tiled=True)

    arrived = returned.transpose(1, 0, 2, 3).reshape(capacity, experts, width)
    mixed, partial_dots = call(
        combine_kernel,
        [((rows, width), BF16), ((top, rows), F32)],
        arrived, cotangent, routes_t, code, code_t, wt,
    )
    dots = broadcast_exchange(partial_dots, CTX)
    partial_router, dlog = call(
        router_kernel,
        [((width, experts), F32), (square, F32)],
        dots, routes_t, small, probs, tokens.T,
    )
    near = lax.axis_size(NEAR)
    mine = lax.all_to_all(
        partial_router.reshape(near, width // near, experts), NEAR, 0, 0, tiled=True
    ).sum(0)
    mine = broadcast_exchange(mine, "z_hi").sum(0)
    router_grad = broadcast_exchange(mine, NEAR).reshape(width, experts)
    token_grad = call(token_grad_kernel, [((rows, width), BF16)], dlog, router_weight)[0]

    first = (lax.axis_index(EXP) * local).astype(jnp.int32).reshape(1)
    slot_grad = owner_rows(everyone, first, sources, capacity, local)
    return (mixed, token_grad, router_grad, slot_grad)


def solution(mesh):
    n = mesh.shape["exp"]
    side = 4 if mesh.shape["ctx"] == 16 else 2
    low = 4 if n == 64 else 2
    split = Mesh(mesh.devices.reshape(side, -1, n // (2 * low), low, 2), CTX + EXP)
    in_specs = (P(EXP, CTX), P(EXP, CTX), P(EXP, None), P(CTX, None), P(EXP, None, CTX))
    out_specs = (P(EXP, CTX), P(EXP, CTX), P(CTX, None), P(EXP, None, CTX))
    return jax.shard_map(step, mesh=split, in_specs=in_specs, out_specs=out_specs, check_vma=False)
```

```python
import functools

import jax
import jax.numpy as jnp
import numpy as np
from jax import lax
from jax.experimental import pallas as pl
from jax.experimental.pallas import tpu as pltpu
from jax.sharding import Mesh
from jax.sharding import PartitionSpec as P


CTX = ("ctx_0", "ctx_1")
FAR = "z_hi"
NEAR = ("z_lo", "core")
EXP = ("z_hi", "z_lo", "core")
F32 = jnp.float32
BF16 = jnp.bfloat16
INTERPRET = False
NT = (((1,), (1,)), ((), ()))
HIGHEST = lax.Precision.HIGHEST


def ring_parts(array, axis):
    size = lax.axis_size(axis)
    parts = [array]
    for shift in range(1, size):
        parts.append(lax.ppermute(array, axis, [(i, (i + shift) % size) for i in range(size)]))
    return parts


def ring_sum(array, axis):
    parts = ring_parts(array, axis)
    total = parts[0]
    for part in parts[1:]:
        total = total + part
    return total


def split3(x):
    hi = x.astype(BF16)
    rest = x - hi.astype(F32)
    mid = rest.astype(BF16)
    lo = (rest - mid.astype(F32)).astype(BF16)
    return hi, mid, lo


def call(kernel, outs, *args, vmem=None):
    vmem = vmem or (False,) * len(args)
    return pl.pallas_call(
        kernel,
        out_shape=[jax.ShapeDtypeStruct(shape, dtype) for shape, dtype in outs],
        in_specs=[pl.BlockSpec(memory_space=pltpu.VMEM) for _ in args],
        out_specs=[pl.BlockSpec(memory_space=pltpu.VMEM) for _ in outs],
        interpret=INTERPRET,
    )(*[a if INTERPRET or not v else pltpu.with_memory_space_constraint(a, pltpu.VMEM) for a, v in zip(args, vmem)])


def pack_kernel(perm_ref, in_ref, out_ref):
    local, _, _ = in_ref.shape
    rows = jnp.concatenate([in_ref[e] for e in range(local)], axis=0)
    out = jnp.dot(perm_ref[...], rows, preferred_element_type=F32).astype(BF16)
    out_ref[...] = out.reshape(out_ref.shape)


def pack_rows(expert_out, sources, capacity):
    local, _, width = expert_out.shape
    group = 8
    span = group * capacity
    perm = np.zeros((local * span, local * span), np.float32)
    for s in range(group):
        for e in range(local):
            for c in range(capacity):
                perm[(s * local + e) * capacity + c, e * span + s * capacity + c] = 1.0
    return pl.pallas_call(
        pack_kernel,
        grid=(sources // group,),
        in_specs=[
            pl.BlockSpec((local * span, local * span), lambda i: (0, 0)),
            pl.BlockSpec((local, span, width), lambda i: (0, i, 0)),
        ],
        out_specs=pl.BlockSpec((group, local * capacity, width), lambda i: (i, 0, 0)),
        out_shape=jax.ShapeDtypeStruct((sources, local * capacity, width), BF16),
        interpret=INTERPRET,
    )(jnp.asarray(perm, BF16), expert_out)


def gate_kernel(capacity, logits_ref, routes_ref, probs_ref, small_ref, row_ref, wt_ref, slots_ref):
    logits = logits_ref[...]
    experts, tokens = logits.shape
    top = routes_ref.shape[0]
    expo = jnp.exp(logits)
    probs = expo / jnp.sum(expo, axis=0, keepdims=True)
    probs_ref[...] = probs
    which = lax.broadcasted_iota(jnp.int32, (experts, tokens), 0)
    hits = [which == routes_ref[k : k + 1, :] for k in range(top)]
    chosen = jnp.concatenate(
        [jnp.sum(jnp.where(hit, probs, 0.0), axis=0, keepdims=True) for hit in hits], axis=0
    )
    total = jnp.sum(chosen, axis=0, keepdims=True)
    gates = chosen / total
    small_ref[0:top, :] = chosen
    small_ref[top : 2 * top, :] = gates
    small_ref[2 * top : 3 * top, :] = jnp.broadcast_to(total, (top, tokens))
    dense = jnp.zeros((experts, tokens), F32)
    member = jnp.zeros((experts, tokens), F32)
    for k in range(top):
        dense = dense + jnp.where(hits[k], gates[k : k + 1, :], 0.0)
        member = member + jnp.where(hits[k], 1.0, 0.0)
    before = lax.broadcasted_iota(jnp.int32, (tokens, tokens), 0)
    after = lax.broadcasted_iota(jnp.int32, (tokens, tokens), 1)
    upper = jnp.where(before < after, 1.0, 0.0).astype(BF16)
    position = jnp.dot(member.astype(BF16), upper, preferred_element_type=F32)
    place = which.astype(F32) * float(capacity) + position
    row = jnp.concatenate(
        [jnp.sum(jnp.where(hit, place, 0.0), axis=0, keepdims=True) for hit in hits], axis=0
    )
    row_ref[...] = row
    row_t = row.T
    gates_t = gates.T
    step = min(128, wt_ref.shape[2])
    for c in range(wt_ref.shape[2] // step):
        lane = lax.broadcasted_iota(jnp.int32, (tokens, step), 1).astype(F32) + float(c * step)
        weight = jnp.zeros((tokens, step), F32)
        for k in range(top):
            weight = weight + jnp.where(lane == row_t[:, k : k + 1], gates_t[:, k : k + 1], 0.0)
        for i, term in enumerate(split3(weight)):
            wt_ref[i, :, c * step : (c + 1) * step] = term
    code = jnp.where(member > 0.5, position, -1.0)
    number = after.astype(F32)[0:1, :] + 1.0
    lane = lax.broadcasted_iota(jnp.int32, (experts, 128), 1)
    odd = lax.broadcasted_iota(jnp.int32, (experts, 128), 0) & 1
    lane = lane - 32 * odd
    table = jnp.zeros((experts, 128), F32)
    for s in range(capacity):
        here = code == float(s)
        gate = jnp.sum(jnp.where(here, dense, 0.0), axis=1, keepdims=True)
        token = jnp.sum(jnp.where(here, number, 0.0), axis=1, keepdims=True)
        table = table + jnp.where(lane == s, gate, 0.0) + jnp.where(lane == 16 + s, token, 0.0)
    near, far, _ = slots_ref.shape
    dest = lax.broadcasted_iota(jnp.int32, (near, far, experts), 1) * near
    dest = dest + lax.broadcasted_iota(jnp.int32, (near, far, experts), 0)
    owner = lax.broadcasted_iota(jnp.int32, (near, far, experts), 2) >> 1
    select = jnp.where(dest == owner, 1.0, 0.0).reshape(near * far, experts).astype(BF16)
    slots = sum(jnp.dot(select, term, preferred_element_type=F32) for term in split3(table))
    slots_ref[...] = slots.reshape(near, far, 128)


def combine_kernel(rows_ref, cot_ref, row_ref, wt_ref, mixed_ref, dots_ref):
    sources, each, width = rows_ref.shape
    cot = cot_ref[...]
    top, tokens = row_ref.shape
    mixed = jnp.zeros((tokens, width), F32)
    group = 8
    span = group * each
    acc = [jnp.zeros((8, tokens), F32) for _ in range(top)]
    index = lax.broadcasted_iota(jnp.int32, (span, tokens), 0).astype(F32)
    for c in range(sources // group):
        rows = rows_ref[c * group : (c + 1) * group].reshape(span, width)
        prod = lax.dot_general(rows, cot, NT, preferred_element_type=F32)
        for k in range(top):
            want = row_ref[k : k + 1, :] - float(c * span)
            part = jnp.where(index == want, prod, 0.0)
            acc[k] = acc[k] + jnp.sum(part.reshape(span // 8, 8, tokens), axis=0)
    dots = jnp.concatenate([jnp.sum(a, axis=0, keepdims=True) for a in acc], axis=0)
    for i in range(dots_ref.shape[0]):
        dots_ref[i] = dots
    rows = rows_ref[...].reshape(sources * each, width)
    for i in range(3):
        mixed = mixed + jnp.dot(wt_ref[i], rows, preferred_element_type=F32)
    mixed_ref[...] = mixed.astype(BF16)


def router_kernel(parts_ref, routes_ref, small_ref, probs_ref, tok_t_ref, slots_ref, part_ref, dlog_ref):
    dots = parts_ref[0]
    for i in range(1, parts_ref.shape[0]):
        dots = dots + parts_ref[i]
    top, _ = dots.shape
    chosen = small_ref[0:top, :]
    gates = small_ref[top : 2 * top, :]
    total = small_ref[2 * top : 3 * top, :]
    dchosen = (dots - jnp.sum(dots * gates, axis=0, keepdims=True)) / total
    level = jnp.sum(chosen * dchosen, axis=0, keepdims=True)
    probs = probs_ref[...]
    which = lax.broadcasted_iota(jnp.int32, probs.shape, 0)
    spread = jnp.zeros(probs.shape, F32)
    for k in range(top):
        spread = spread + jnp.where(which == routes_ref[k : k + 1, :], dchosen[k : k + 1, :], 0.0)
    dlog = probs * (spread - level)
    tok_t = tok_t_ref[...]
    acc = None
    for term in split3(dlog):
        one = lax.dot_general(tok_t, term, NT, preferred_element_type=F32)
        acc = one if acc is None else acc + one
    near, far, _ = slots_ref.shape
    share = acc.shape[0] // near
    for n in range(near):
        part_ref[n, 0:share, :] = acc[n * share : (n + 1) * share, :]
        part_ref[n, share : share + far, :] = slots_ref[n]
    dlog_ref[...] = dlog


def near_kernel(in_ref, out_ref):
    near = in_ref.shape[0]
    far = out_ref.shape[0]
    share = in_ref.shape[1] - far
    total = in_ref[0, 0:share, :]
    for n in range(1, near):
        total = total + in_ref[n, 0:share, :]
    for f in range(far):
        out_ref[f, 0:share, :] = total
        for n in range(near):
            out_ref[f, share + n : share + n + 1, :] = in_ref[n, share + f : share + f + 1, :]


def far_kernel(in_ref, out_ref):
    far = in_ref.shape[0]
    share = out_ref.shape[1]
    total = in_ref[0, 0:share, :]
    for f in range(1, far):
        total = total + in_ref[f, 0:share, :]
    for n in range(out_ref.shape[0]):
        out_ref[n] = total


def token_grad_kernel(dlog_ref, weight_ref, out_ref):
    out_ref[...] = lax.dot_general(
        dlog_ref[...].T, weight_ref[...], NT, precision=HIGHEST, preferred_element_type=F32
    ).astype(BF16)


def owner_kernel(capacity, near, tokens, slots_ref, all_ref, out_ref):
    local = out_ref.shape[0]
    share = slots_ref.shape[1] - near
    group = 4
    rows = group * capacity
    index = lax.broadcasted_iota(jnp.int32, (rows, 128), 0)
    source = sum(jnp.where(index >= q * capacity, 1, 0) for q in range(1, group))
    slot = index - capacity * source
    lane = lax.broadcasted_iota(jnp.int32, (rows, 128), 1)
    column = lax.broadcasted_iota(jnp.int32, (rows, group * tokens), 1).astype(F32)
    base = (source[:, 0:1] * tokens).astype(F32)
    for h in range(near // group):
        at = share + h * group
        table = jnp.broadcast_to(slots_ref[0, at : at + 1, :], (rows, 128))
        for q in range(1, group):
            table = jnp.where(source == q, slots_ref[0, at + q : at + q + 1, :], table)
        gates, picks = [], []
        for e in range(local):
            gates.append(jnp.sum(jnp.where(lane == slot + 32 * e, table, 0.0), axis=1, keepdims=True))
            token = jnp.sum(jnp.where(lane == slot + 32 * e + 16, table, 0.0), axis=1, keepdims=True)
            want = jnp.where(token > 0.5, token - 1.0 + base, -1.0)
            picks.append(jnp.where(column == want, 1.0, 0.0).astype(BF16))
        cot = all_ref[h * group * tokens : (h + 1) * group * tokens, :]
        picked = jnp.dot(jnp.concatenate(picks, axis=0), cot, preferred_element_type=F32)
        for e in range(local):
            out_ref[e, h * rows : (h + 1) * rows, :] = (
                gates[e] * picked[e * rows : (e + 1) * rows, :]
            ).astype(BF16)


def owner_rows(everyone, slots, capacity, near, local):
    far, height, _ = slots.shape
    count, width = everyone.shape
    tokens = count // (far * near)
    return pl.pallas_call(
        functools.partial(owner_kernel, capacity, near, tokens),
        grid=(far,),
        in_specs=[
            pl.BlockSpec((1, height, 128), lambda i: (i, 0, 0)),
            pl.BlockSpec((near * tokens, width), lambda i: (i, 0)),
        ],
        out_specs=pl.BlockSpec((local, near * capacity, width), lambda i: (0, i, 0)),
        out_shape=jax.ShapeDtypeStruct((local, far * near * capacity, width), BF16),
        interpret=INTERPRET,
    )(slots, everyone)


def step(tokens, cotangent, routes, router_weight, expert_out):
    rows, top = routes.shape
    local = expert_out.shape[0]
    sources = lax.axis_size(EXP)
    near = lax.axis_size(NEAR)
    far = lax.axis_size(FAR)
    experts = local * sources
    capacity = expert_out.shape[1] // sources
    width = tokens.shape[1]
    share = width // near
    routes_t = routes.T

    everyone = lax.all_gather(cotangent, EXP, tiled=True)
    sent = pack_rows(expert_out, sources, capacity)
    arrived = lax.all_to_all(sent, EXP, 0, 0, tiled=True)

    partial_logits = lax.dot_general(
        router_weight, tokens.astype(F32), (((0,), (1,)), ((), ())), precision=HIGHEST
    )
    logits = ring_sum(partial_logits, CTX[1])
    logits = ring_sum(logits, CTX[0])
    square = (experts, rows)
    probs, small, row, wt, slots = call(
        functools.partial(gate_kernel, capacity),
        [
            (square, F32),
            ((3 * top, rows), F32),
            ((top, rows), F32),
            ((3, rows, experts * capacity), BF16),
            ((near, far, 128), F32),
        ],
        logits, routes_t,
    )

    mixed, partial_dots = call(
        combine_kernel,
        [((rows, width), BF16), ((lax.axis_size(CTX), top, rows), F32)],
        arrived, cotangent, row, wt,
        vmem=(True, False, True, True),
    )
    dots = lax.all_to_all(partial_dots, CTX, 0, 0, tiled=True)
    partial_router, dlog = call(
        router_kernel,
        [((near, share + far, experts), F32), (square, F32)],
        dots, routes_t, small, probs, tokens.T, slots,
        vmem=(True, False, True, True, True, True),
    )
    partial_router = lax.all_to_all(partial_router, NEAR, 0, 0, tiled=True)
    mine = call(near_kernel, [((far, share + near, experts), F32)], partial_router, vmem=(True,))[0]
    mine = lax.all_to_all(mine, FAR, 0, 0, tiled=True)
    total = call(far_kernel, [((near, share, experts), F32)], mine, vmem=(True,))[0]
    router_grad = lax.all_to_all(total, NEAR, 0, 0, tiled=True).reshape(width, experts)
    token_grad = call(token_grad_kernel, [((rows, width), BF16)], dlog, router_weight)[0]
    slot_grad = owner_rows(everyone, mine, capacity, near, local)
    return (mixed, token_grad, router_grad, slot_grad)


def solution(mesh):
    n = mesh.shape["exp"]
    side = 4 if mesh.shape["ctx"] == 16 else 2
    low = 4 if n == 64 else 2
    split = Mesh(mesh.devices.reshape(side, -1, n // (2 * low), low, 2), CTX + EXP)
    in_specs = (P(EXP, CTX), P(EXP, CTX), P(EXP, None), P(CTX, None), P(EXP, None, CTX))
    out_specs = (P(EXP, CTX), P(EXP, CTX), P(CTX, None), P(EXP, None, CTX))
    return jax.shard_map(step, mesh=split, in_specs=in_specs, out_specs=out_specs, check_vma=False)
```

```python
import functools

import jax
import jax.numpy as jnp
import numpy as np
from jax import lax
from jax.experimental import pallas as pl
from jax.experimental.pallas import tpu as pltpu
from jax.sharding import Mesh
from jax.sharding import PartitionSpec as P


CTX = ("ctx_0", "ctx_1")
FAR = "z_hi"
NEAR = ("z_lo", "core")
EXP = ("z_hi", "z_lo", "core")
F32 = jnp.float32
BF16 = jnp.bfloat16
INTERPRET = False
NT = (((1,), (1,)), ((), ()))
HIGHEST = lax.Precision.HIGHEST


def ring_parts(array, axis):
    size = lax.axis_size(axis)
    parts = [array]
    for shift in range(1, size):
        parts.append(lax.ppermute(array, axis, [(i, (i + shift) % size) for i in range(size)]))
    return parts


def ring_sum(array, axis):
    parts = ring_parts(array, axis)
    total = parts[0]
    for part in parts[1:]:
        total = total + part
    return total


def split3(x):
    hi = x.astype(BF16)
    rest = x - hi.astype(F32)
    mid = rest.astype(BF16)
    lo = (rest - mid.astype(F32)).astype(BF16)
    return hi, mid, lo


def near_memory(array):
    return array if INTERPRET else pltpu.with_memory_space_constraint(array, pltpu.VMEM)


def shaped(shape, dtype, vmem):
    return pltpu.VMEM(shape, dtype) if vmem and not INTERPRET else jax.ShapeDtypeStruct(shape, dtype)


def call(kernel, outs, *args, vmem=None):
    vmem = vmem or (False,) * len(args)
    return pl.pallas_call(
        kernel,
        out_shape=[shaped(*out) for out in outs],
        in_specs=[pl.BlockSpec(memory_space=pltpu.VMEM) for _ in args],
        out_specs=[pl.BlockSpec(memory_space=pltpu.VMEM) for _ in outs],
        interpret=INTERPRET,
    )(*[near_memory(a) if v else a for a, v in zip(args, vmem)])


def pack_kernel(perm_ref, in_ref, out_ref):
    local, _, width = in_ref.shape
    dests, each, _ = out_ref.shape
    span = perm_ref.shape[0] // local
    group = span * local // each
    perm = perm_ref[...]
    for c in range(dests // group):
        rows = jnp.concatenate([in_ref[e, c * span : (c + 1) * span, :] for e in range(local)], axis=0)
        out = jnp.dot(perm, rows, preferred_element_type=F32).astype(BF16)
        out_ref[c * group : (c + 1) * group] = out.reshape(group, each, width)


def pack_rows(expert_out, sources, capacity):
    local, _, width = expert_out.shape
    group = 8
    span = group * capacity
    perm = np.zeros((local * span, local * span), np.float32)
    for s in range(group):
        for e in range(local):
            for c in range(capacity):
                perm[(s * local + e) * capacity + c, e * span + s * capacity + c] = 1.0
    return call(
        pack_kernel,
        [((sources, local * capacity, width), BF16, True)],
        jnp.asarray(perm, BF16), expert_out,
    )[0]


def gate_kernel(capacity, logits_ref, routes_ref, probs_ref, small_ref, row_ref, wt_ref, slots_ref):
    logits = logits_ref[...]
    experts, tokens = logits.shape
    top = routes_ref.shape[0]
    expo = jnp.exp(logits)
    probs = expo / jnp.sum(expo, axis=0, keepdims=True)
    probs_ref[...] = probs
    which = lax.broadcasted_iota(jnp.int32, (experts, tokens), 0)
    hits = [which == routes_ref[k : k + 1, :] for k in range(top)]
    chosen = jnp.concatenate(
        [jnp.sum(jnp.where(hit, probs, 0.0), axis=0, keepdims=True) for hit in hits], axis=0
    )
    total = jnp.sum(chosen, axis=0, keepdims=True)
    gates = chosen / total
    small_ref[0:top, :] = chosen
    small_ref[top : 2 * top, :] = gates
    small_ref[2 * top : 3 * top, :] = jnp.broadcast_to(total, (top, tokens))
    dense = jnp.zeros((experts, tokens), F32)
    member = jnp.zeros((experts, tokens), F32)
    for k in range(top):
        dense = dense + jnp.where(hits[k], gates[k : k + 1, :], 0.0)
        member = member + jnp.where(hits[k], 1.0, 0.0)
    before = lax.broadcasted_iota(jnp.int32, (tokens, tokens), 0)
    after = lax.broadcasted_iota(jnp.int32, (tokens, tokens), 1)
    upper = jnp.where(before < after, 1.0, 0.0).astype(BF16)
    position = jnp.dot(member.astype(BF16), upper, preferred_element_type=F32)
    place = which.astype(F32) * float(capacity) + position
    row = jnp.concatenate(
        [jnp.sum(jnp.where(hit, place, 0.0), axis=0, keepdims=True) for hit in hits], axis=0
    )
    row_ref[...] = row
    row_t = row.T
    gates_t = gates.T
    step = min(128, wt_ref.shape[2])
    for c in range(wt_ref.shape[2] // step):
        lane = lax.broadcasted_iota(jnp.int32, (tokens, step), 1).astype(F32) + float(c * step)
        weight = jnp.zeros((tokens, step), F32)
        for k in range(top):
            weight = weight + jnp.where(lane == row_t[:, k : k + 1], gates_t[:, k : k + 1], 0.0)
        for i, term in enumerate(split3(weight)):
            wt_ref[i, :, c * step : (c + 1) * step] = term
    code = jnp.where(member > 0.5, position, -1.0)
    number = after.astype(F32)[0:1, :] + 1.0
    lane = lax.broadcasted_iota(jnp.int32, (experts, 128), 1)
    odd = lax.broadcasted_iota(jnp.int32, (experts, 128), 0) & 1
    lane = lane - 32 * odd
    table = jnp.zeros((experts, 128), F32)
    for s in range(capacity):
        here = code == float(s)
        gate = jnp.sum(jnp.where(here, dense, 0.0), axis=1, keepdims=True)
        token = jnp.sum(jnp.where(here, number, 0.0), axis=1, keepdims=True)
        table = table + jnp.where(lane == s, gate, 0.0) + jnp.where(lane == 16 + s, token, 0.0)
    near, far, _ = slots_ref.shape
    dest = lax.broadcasted_iota(jnp.int32, (near, far, experts), 1) * near
    dest = dest + lax.broadcasted_iota(jnp.int32, (near, far, experts), 0)
    owner = lax.broadcasted_iota(jnp.int32, (near, far, experts), 2) >> 1
    select = jnp.where(dest == owner, 1.0, 0.0).reshape(near * far, experts).astype(BF16)
    slots = sum(jnp.dot(select, term, preferred_element_type=F32) for term in split3(table))
    slots_ref[...] = slots.reshape(near, far, 128)


def combine_kernel(rows_ref, cot_ref, row_ref, wt_ref, mixed_ref, dots_ref):
    sources, each, width = rows_ref.shape
    cot = cot_ref[...]
    top, tokens = row_ref.shape
    mixed = jnp.zeros((tokens, width), F32)
    group = 8
    span = group * each
    acc = [jnp.zeros((8, tokens), F32) for _ in range(top)]
    index = lax.broadcasted_iota(jnp.int32, (span, tokens), 0).astype(F32)
    for c in range(sources // group):
        rows = rows_ref[c * group : (c + 1) * group].reshape(span, width)
        prod = lax.dot_general(rows, cot, NT, preferred_element_type=F32)
        for k in range(top):
            want = row_ref[k : k + 1, :] - float(c * span)
            part = jnp.where(index == want, prod, 0.0)
            acc[k] = acc[k] + jnp.sum(part.reshape(span // 8, 8, tokens), axis=0)
    dots = jnp.concatenate([jnp.sum(a, axis=0, keepdims=True) for a in acc], axis=0)
    for i in range(dots_ref.shape[0]):
        dots_ref[i] = dots
    rows = rows_ref[...].reshape(sources * each, width)
    for i in range(3):
        mixed = mixed + jnp.dot(wt_ref[i], rows, preferred_element_type=F32)
    mixed_ref[...] = mixed.astype(BF16)


def router_kernel(parts_ref, routes_ref, small_ref, probs_ref, tok_t_ref, slots_ref, part_ref, dlog_ref):
    dots = parts_ref[0]
    for i in range(1, parts_ref.shape[0]):
        dots = dots + parts_ref[i]
    top, _ = dots.shape
    chosen = small_ref[0:top, :]
    gates = small_ref[top : 2 * top, :]
    total = small_ref[2 * top : 3 * top, :]
    dchosen = (dots - jnp.sum(dots * gates, axis=0, keepdims=True)) / total
    level = jnp.sum(chosen * dchosen, axis=0, keepdims=True)
    probs = probs_ref[...]
    which = lax.broadcasted_iota(jnp.int32, probs.shape, 0)
    spread = jnp.zeros(probs.shape, F32)
    for k in range(top):
        spread = spread + jnp.where(which == routes_ref[k : k + 1, :], dchosen[k : k + 1, :], 0.0)
    dlog = probs * (spread - level)
    tok_t = tok_t_ref[...]
    acc = None
    for term in split3(dlog):
        one = lax.dot_general(tok_t, term, NT, preferred_element_type=F32)
        acc = one if acc is None else acc + one
    near, far, _ = slots_ref.shape
    share = acc.shape[0] // near
    for n in range(near):
        part_ref[n, 0:share, :] = acc[n * share : (n + 1) * share, :]
        part_ref[n, share : share + far, :] = slots_ref[n]
    dlog_ref[...] = dlog


def near_kernel(in_ref, out_ref):
    near = in_ref.shape[0]
    far = out_ref.shape[0]
    share = in_ref.shape[1] - far
    total = in_ref[0, 0:share, :]
    for n in range(1, near):
        total = total + in_ref[n, 0:share, :]
    for f in range(far):
        out_ref[f, 0:share, :] = total
        for n in range(near):
            out_ref[f, share + n : share + n + 1, :] = in_ref[n, share + f : share + f + 1, :]


def far_kernel(in_ref, out_ref):
    far = in_ref.shape[0]
    share = out_ref.shape[1]
    total = in_ref[0, 0:share, :]
    for f in range(1, far):
        total = total + in_ref[f, 0:share, :]
    for n in range(out_ref.shape[0]):
        out_ref[n] = total


def token_grad_kernel(dlog_ref, weight_ref, out_ref):
    out_ref[...] = lax.dot_general(
        dlog_ref[...].T, weight_ref[...], NT, precision=HIGHEST, preferred_element_type=F32
    ).astype(BF16)


def owner_kernel(capacity, near, tokens, slots_ref, all_ref, out_ref):
    step = pl.program_id(0)
    local = out_ref.shape[0]
    share = slots_ref.shape[1] - near
    group = 4
    rows = group * capacity
    index = lax.broadcasted_iota(jnp.int32, (rows, 128), 0)
    source = sum(jnp.where(index >= q * capacity, 1, 0) for q in range(1, group))
    slot = index - capacity * source
    lane = lax.broadcasted_iota(jnp.int32, (rows, 128), 1)
    column = lax.broadcasted_iota(jnp.int32, (rows, group * tokens), 1).astype(F32)
    base = (source[:, 0:1] * tokens).astype(F32)
    for h in range(near // group):
        at = share + h * group
        table = jnp.broadcast_to(slots_ref[step, at : at + 1, :], (rows, 128))
        for q in range(1, group):
            table = jnp.where(source == q, slots_ref[step, at + q : at + q + 1, :], table)
        gates, picks = [], []
        for e in range(local):
            gates.append(jnp.sum(jnp.where(lane == slot + 32 * e, table, 0.0), axis=1, keepdims=True))
            token = jnp.sum(jnp.where(lane == slot + 32 * e + 16, table, 0.0), axis=1, keepdims=True)
            want = jnp.where(token > 0.5, token - 1.0 + base, -1.0)
            picks.append(jnp.where(column == want, 1.0, 0.0).astype(BF16))
        cot = all_ref[h * group * tokens : (h + 1) * group * tokens, :]
        picked = jnp.dot(jnp.concatenate(picks, axis=0), cot, preferred_element_type=F32)
        for e in range(local):
            out_ref[e, h * rows : (h + 1) * rows, :] = (
                gates[e] * picked[e * rows : (e + 1) * rows, :]
            ).astype(BF16)


def owner_rows(everyone, slots, capacity, near, local):
    far, _, _ = slots.shape
    count, width = everyone.shape
    tokens = count // (far * near)
    return pl.pallas_call(
        functools.partial(owner_kernel, capacity, near, tokens),
        grid=(far,),
        in_specs=[
            pl.BlockSpec(memory_space=pltpu.VMEM),
            pl.BlockSpec((near * tokens, width), lambda i: (i, 0)),
        ],
        out_specs=pl.BlockSpec((local, near * capacity, width), lambda i: (0, i, 0)),
        out_shape=jax.ShapeDtypeStruct((local, far * near * capacity, width), BF16),
        interpret=INTERPRET,
    )(near_memory(slots), everyone)


def step(tokens, cotangent, routes, router_weight, expert_out):
    rows, top = routes.shape
    local = expert_out.shape[0]
    sources = lax.axis_size(EXP)
    near = lax.axis_size(NEAR)
    far = lax.axis_size(FAR)
    experts = local * sources
    capacity = expert_out.shape[1] // sources
    width = tokens.shape[1]
    share = width // near
    routes_t = routes.T

    everyone = lax.all_gather(cotangent, EXP, tiled=True)
    sent = pack_rows(expert_out, sources, capacity)
    arrived = lax.all_to_all(sent, EXP, 0, 0, tiled=True)

    partial_logits = lax.dot_general(
        router_weight, tokens.astype(F32), (((0,), (1,)), ((), ())), precision=HIGHEST
    )
    logits = ring_sum(partial_logits, CTX[1])
    logits = ring_sum(logits, CTX[0])
    square = (experts, rows)
    probs, small, row, wt, slots = call(
        functools.partial(gate_kernel, capacity),
        [
            (square, F32, True),
            ((3 * top, rows), F32, True),
            ((top, rows), F32, True),
            ((3, rows, experts * capacity), BF16, True),
            ((near, far, 128), F32, True),
        ],
        logits, routes_t,
    )

    mixed, partial_dots = call(
        combine_kernel,
        [((rows, width), BF16, False), ((lax.axis_size(CTX), top, rows), F32, True)],
        arrived, cotangent, row, wt,
        vmem=(True, False, True, True),
    )
    dots = lax.all_to_all(partial_dots, CTX, 0, 0, tiled=True)
    partial_router, dlog = call(
        router_kernel,
        [((near, share + far, experts), F32, True), (square, F32, True)],
        dots, routes_t, small, probs, tokens.T, slots,
        vmem=(True, False, True, True, True, True),
    )
    partial_router = lax.all_to_all(partial_router, NEAR, 0, 0, tiled=True)
    mine = call(near_kernel, [((far, share + near, experts), F32, True)], partial_router, vmem=(True,))[0]
    mine = lax.all_to_all(mine, FAR, 0, 0, tiled=True)
    total = call(far_kernel, [((near, share, experts), F32, True)], mine, vmem=(True,))[0]
    router_grad = lax.all_to_all(total, NEAR, 0, 0, tiled=True).reshape(width, experts)
    token_grad = call(
        token_grad_kernel, [((rows, width), BF16, False)], dlog, router_weight, vmem=(True, False)
    )[0]
    slot_grad = owner_rows(everyone, mine, capacity, near, local)
    return (mixed, token_grad, router_grad, slot_grad)


def solution(mesh):
    n = mesh.shape["exp"]
    side = 4 if mesh.shape["ctx"] == 16 else 2
    low = 4 if n == 64 else 2
    split = Mesh(mesh.devices.reshape(side, -1, n // (2 * low), low, 2), CTX + EXP)
    in_specs = (P(EXP, CTX), P(EXP, CTX), P(EXP, None), P(CTX, None), P(EXP, None, CTX))
    out_specs = (P(EXP, CTX), P(EXP, CTX), P(CTX, None), P(EXP, None, CTX))
    return jax.shard_map(step, mesh=split, in_specs=in_specs, out_specs=out_specs, check_vma=False)
```

```python
import functools

import jax
import jax.numpy as jnp
import numpy as np
from jax import lax
from jax.experimental import pallas as pl
from jax.experimental.pallas import tpu as pltpu
from jax.sharding import Mesh
from jax.sharding import PartitionSpec as P


CTX = ("ctx_0", "ctx_1")
FAR = "z_hi"
NEAR = ("z_lo", "core")
EXP = ("z_hi", "z_lo", "core")
SPREAD = ("z_lo", "z_hi", "core")
F32 = jnp.float32
BF16 = jnp.bfloat16
INTERPRET = False
NT = (((1,), (1,)), ((), ()))
HIGHEST = lax.Precision.HIGHEST


def ring_parts(array, axis):
    size = lax.axis_size(axis)
    parts = [array]
    for shift in range(1, size):
        parts.append(lax.ppermute(array, axis, [(i, (i + shift) % size) for i in range(size)]))
    return parts


def ring_sum(array, axis):
    parts = ring_parts(array, axis)
    total = parts[0]
    for part in parts[1:]:
        total = total + part
    return total


def split3(x):
    hi = x.astype(BF16)
    rest = x - hi.astype(F32)
    mid = rest.astype(BF16)
    lo = (rest - mid.astype(F32)).astype(BF16)
    return hi, mid, lo


def near_memory(array):
    return array if INTERPRET else pltpu.with_memory_space_constraint(array, pltpu.VMEM)


def shaped(shape, dtype, vmem):
    return pltpu.VMEM(shape, dtype) if vmem and not INTERPRET else jax.ShapeDtypeStruct(shape, dtype)


def call(kernel, outs, *args, vmem=None):
    vmem = vmem or (False,) * len(args)
    return pl.pallas_call(
        kernel,
        out_shape=[shaped(*out) for out in outs],
        in_specs=[pl.BlockSpec(memory_space=pltpu.VMEM) for _ in args],
        out_specs=[pl.BlockSpec(memory_space=pltpu.VMEM) for _ in outs],
        interpret=INTERPRET,
    )(*[near_memory(a) if v else a for a, v in zip(args, vmem)])


def pack_kernel(perm_ref, in_ref, out_ref):
    local, _, width = in_ref.shape
    dests, each, _ = out_ref.shape
    span = perm_ref.shape[0] // local
    group = span * local // each
    perm = perm_ref[...]
    for c in range(dests // group):
        rows = jnp.concatenate([in_ref[e, c * span : (c + 1) * span, :] for e in range(local)], axis=0)
        out = jnp.dot(perm, rows, preferred_element_type=F32).astype(BF16)
        out = out.reshape(group, each, width)
        for low in range(group // 2):
            at = low * 2 * (dests // group) + 2 * c
            out_ref[at : at + 2] = out[2 * low : 2 * low + 2]


def pack_rows(expert_out, sources, capacity, group):
    local, _, width = expert_out.shape
    span = group * capacity
    perm = np.zeros((local * span, local * span), np.float32)
    for s in range(group):
        for e in range(local):
            for c in range(capacity):
                perm[(s * local + e) * capacity + c, e * span + s * capacity + c] = 1.0
    return call(
        pack_kernel,
        [((sources, local * capacity, width), BF16, True)],
        jnp.asarray(perm, BF16), expert_out,
    )[0]


def gate_kernel(capacity, logits_ref, routes_ref, probs_ref, small_ref, row_ref, wt_ref, slots_ref):
    logits = logits_ref[...]
    experts, tokens = logits.shape
    top = routes_ref.shape[0]
    expo = jnp.exp(logits)
    probs = expo / jnp.sum(expo, axis=0, keepdims=True)
    probs_ref[...] = probs
    which = lax.broadcasted_iota(jnp.int32, (experts, tokens), 0)
    hits = [which == routes_ref[k : k + 1, :] for k in range(top)]
    chosen = jnp.concatenate(
        [jnp.sum(jnp.where(hit, probs, 0.0), axis=0, keepdims=True) for hit in hits], axis=0
    )
    total = jnp.sum(chosen, axis=0, keepdims=True)
    gates = chosen / total
    small_ref[0:top, :] = chosen
    small_ref[top : 2 * top, :] = gates
    small_ref[2 * top : 3 * top, :] = jnp.broadcast_to(total, (top, tokens))
    dense = jnp.zeros((experts, tokens), F32)
    member = jnp.zeros((experts, tokens), F32)
    for k in range(top):
        dense = dense + jnp.where(hits[k], gates[k : k + 1, :], 0.0)
        member = member + jnp.where(hits[k], 1.0, 0.0)
    before = lax.broadcasted_iota(jnp.int32, (tokens, tokens), 0)
    after = lax.broadcasted_iota(jnp.int32, (tokens, tokens), 1)
    upper = jnp.where(before < after, 1.0, 0.0).astype(BF16)
    position = jnp.dot(member.astype(BF16), upper, preferred_element_type=F32)
    near, far, _ = slots_ref.shape
    span = experts // far
    high, rest = which // span, which % span
    order = (rest // 4) * (4 * far) + high * 4 + rest % 4
    place = order.astype(F32) * float(capacity) + position
    row = jnp.concatenate(
        [jnp.sum(jnp.where(hit, place, 0.0), axis=0, keepdims=True) for hit in hits], axis=0
    )
    row_ref[...] = row
    row_t = row.T
    gates_t = gates.T
    step = min(128, wt_ref.shape[2])
    for c in range(wt_ref.shape[2] // step):
        lane = lax.broadcasted_iota(jnp.int32, (tokens, step), 1).astype(F32) + float(c * step)
        weight = jnp.zeros((tokens, step), F32)
        for k in range(top):
            weight = weight + jnp.where(lane == row_t[:, k : k + 1], gates_t[:, k : k + 1], 0.0)
        for i, term in enumerate(split3(weight)):
            wt_ref[i, :, c * step : (c + 1) * step] = term
    code = jnp.where(member > 0.5, position, -1.0)
    number = after.astype(F32)[0:1, :] + 1.0
    lane = lax.broadcasted_iota(jnp.int32, (experts, 128), 1)
    odd = lax.broadcasted_iota(jnp.int32, (experts, 128), 0) & 1
    lane = lane - 32 * odd
    table = jnp.zeros((experts, 128), F32)
    for s in range(capacity):
        here = code == float(s)
        gate = jnp.sum(jnp.where(here, dense, 0.0), axis=1, keepdims=True)
        token = jnp.sum(jnp.where(here, number, 0.0), axis=1, keepdims=True)
        table = table + jnp.where(lane == s, gate, 0.0) + jnp.where(lane == 16 + s, token, 0.0)
    dest = lax.broadcasted_iota(jnp.int32, (near, far, experts), 1) * near
    dest = dest + lax.broadcasted_iota(jnp.int32, (near, far, experts), 0)
    owner = lax.broadcasted_iota(jnp.int32, (near, far, experts), 2) >> 1
    select = jnp.where(dest == owner, 1.0, 0.0).reshape(near * far, experts).astype(BF16)
    slots = sum(jnp.dot(select, term, preferred_element_type=F32) for term in split3(table))
    slots_ref[...] = slots.reshape(near, far, 128)


def dots_kernel(rows_ref, cot_ref, row_ref, dots_ref):
    sources, each, width = rows_ref.shape
    cot = cot_ref[...]
    top, tokens = row_ref.shape
    group = 8
    span = group * each
    acc = [jnp.zeros((8, tokens), F32) for _ in range(top)]
    index = lax.broadcasted_iota(jnp.int32, (span, tokens), 0).astype(F32)
    for c in range(sources // group):
        rows = rows_ref[c * group : (c + 1) * group].reshape(span, width)
        prod = lax.dot_general(rows, cot, NT, preferred_element_type=F32)
        for k in range(top):
            want = row_ref[k : k + 1, :] - float(c * span)
            part = jnp.where(index == want, prod, 0.0)
            acc[k] = acc[k] + jnp.sum(part.reshape(span // 8, 8, tokens), axis=0)
    dots = jnp.concatenate([jnp.sum(a, axis=0, keepdims=True) for a in acc], axis=0)
    for i in range(dots_ref.shape[0]):
        dots_ref[i] = dots


def mixed_kernel(rows_ref, wt_ref, mixed_ref):
    sources, each, width = rows_ref.shape
    rows = rows_ref[...].reshape(sources * each, width)
    mixed = jnp.dot(wt_ref[0], rows, preferred_element_type=F32)
    for i in range(1, 3):
        mixed = mixed + jnp.dot(wt_ref[i], rows, preferred_element_type=F32)
    mixed_ref[...] = mixed.astype(BF16)


def router_kernel(parts_ref, routes_ref, small_ref, probs_ref, tok_t_ref, slots_ref, part_ref, dlog_ref):
    dots = parts_ref[0]
    for i in range(1, parts_ref.shape[0]):
        dots = dots + parts_ref[i]
    top, _ = dots.shape
    chosen = small_ref[0:top, :]
    gates = small_ref[top : 2 * top, :]
    total = small_ref[2 * top : 3 * top, :]
    dchosen = (dots - jnp.sum(dots * gates, axis=0, keepdims=True)) / total
    level = jnp.sum(chosen * dchosen, axis=0, keepdims=True)
    probs = probs_ref[...]
    which = lax.broadcasted_iota(jnp.int32, probs.shape, 0)
    spread = jnp.zeros(probs.shape, F32)
    for k in range(top):
        spread = spread + jnp.where(which == routes_ref[k : k + 1, :], dchosen[k : k + 1, :], 0.0)
    dlog = probs * (spread - level)
    tok_t = tok_t_ref[...]
    acc = None
    for term in split3(dlog):
        one = lax.dot_general(tok_t, term, NT, preferred_element_type=F32)
        acc = one if acc is None else acc + one
    near, far, _ = slots_ref.shape
    share = acc.shape[0] // near
    for n in range(near):
        part_ref[n, 0:share, :] = acc[n * share : (n + 1) * share, :]
        part_ref[n, share : share + far, :] = slots_ref[n]
    dlog_ref[...] = dlog


def near_kernel(in_ref, out_ref):
    near = in_ref.shape[0]
    far = out_ref.shape[0]
    share = in_ref.shape[1] - far
    total = in_ref[0, 0:share, :]
    for n in range(1, near):
        total = total + in_ref[n, 0:share, :]
    for f in range(far):
        out_ref[f, 0:share, :] = total
        for n in range(near):
            out_ref[f, share + n : share + n + 1, :] = in_ref[n, share + f : share + f + 1, :]


def far_kernel(in_ref, out_ref):
    far = in_ref.shape[0]
    share = out_ref.shape[1]
    total = in_ref[0, 0:share, :]
    for f in range(1, far):
        total = total + in_ref[f, 0:share, :]
    for n in range(out_ref.shape[0]):
        out_ref[n] = total


def token_grad_kernel(dlog_ref, weight_ref, out_ref):
    out_ref[...] = lax.dot_general(
        dlog_ref[...].T, weight_ref[...], NT, precision=HIGHEST, preferred_element_type=F32
    ).astype(BF16)


def owner_kernel(capacity, near, tokens, pair, slots_ref, all_ref, out_ref):
    local = out_ref.shape[0]
    share = slots_ref.shape[1] - near
    group = 4
    rows = group * capacity
    index = lax.broadcasted_iota(jnp.int32, (rows, 128), 0)
    source = sum(jnp.where(index >= q * capacity, 1, 0) for q in range(1, group))
    slot = index - capacity * source
    lane = lax.broadcasted_iota(jnp.int32, (rows, 128), 1)
    column = lax.broadcasted_iota(jnp.int32, (rows, group * tokens), 1).astype(F32)
    base = (source[:, 0:1] * tokens).astype(F32)
    for h in range(pair * near // group):
        step = pl.program_id(0) * pair + h * group // near
        at = share + h * group % near
        table = jnp.broadcast_to(slots_ref[step, at : at + 1, :], (rows, 128))
        for q in range(1, group):
            table = jnp.where(source == q, slots_ref[step, at + q : at + q + 1, :], table)
        gates, picks = [], []
        for e in range(local):
            gates.append(jnp.sum(jnp.where(lane == slot + 32 * e, table, 0.0), axis=1, keepdims=True))
            token = jnp.sum(jnp.where(lane == slot + 32 * e + 16, table, 0.0), axis=1, keepdims=True)
            want = jnp.where(token > 0.5, token - 1.0 + base, -1.0)
            picks.append(jnp.where(column == want, 1.0, 0.0).astype(BF16))
        cot = all_ref[h * group * tokens : (h + 1) * group * tokens, :]
        picked = jnp.dot(jnp.concatenate(picks, axis=0), cot, preferred_element_type=F32)
        for e in range(local):
            out_ref[e, h * rows : (h + 1) * rows, :] = (
                gates[e] * picked[e * rows : (e + 1) * rows, :]
            ).astype(BF16)


def owner_rows(everyone, slots, capacity, near, local):
    far = slots.shape[0]
    count, width = everyone.shape
    tokens = count // (far * near)
    pair = 2
    return pl.pallas_call(
        functools.partial(owner_kernel, capacity, near, tokens, pair),
        grid=(far // pair,),
        in_specs=[
            pl.BlockSpec(memory_space=pltpu.VMEM),
            pl.BlockSpec((pair * near * tokens, width), lambda i: (i, 0)),
        ],
        out_specs=pl.BlockSpec((local, pair * near * capacity, width), lambda i: (0, i, 0)),
        out_shape=jax.ShapeDtypeStruct((local, far * near * capacity, width), BF16),
        interpret=INTERPRET,
    )(near_memory(slots), everyone)


def step(tokens, cotangent, routes, router_weight, expert_out):
    rows, top = routes.shape
    local = expert_out.shape[0]
    sources = lax.axis_size(EXP)
    near = lax.axis_size(NEAR)
    far = lax.axis_size(FAR)
    experts = local * sources
    capacity = expert_out.shape[1] // sources
    width = tokens.shape[1]
    share = width // near
    routes_t = routes.T

    everyone = lax.all_gather(cotangent, EXP, tiled=True)
    sent = pack_rows(expert_out, sources, capacity, near)
    arrived = lax.all_to_all(sent, SPREAD, 0, 0, tiled=True)

    partial_logits = lax.dot_general(
        router_weight, tokens.astype(F32), (((0,), (1,)), ((), ())), precision=HIGHEST
    )
    logits = ring_sum(partial_logits, CTX[1])
    logits = ring_sum(logits, CTX[0])
    square = (experts, rows)
    probs, small, row, wt, slots = call(
        functools.partial(gate_kernel, capacity),
        [
            (square, F32, True),
            ((3 * top, rows), F32, True),
            ((top, rows), F32, True),
            ((3, rows, experts * capacity), BF16, False),
            ((near, far, 128), F32, True),
        ],
        logits, routes_t,
    )

    partial_dots = call(
        dots_kernel,
        [((lax.axis_size(CTX), top, rows), F32, True)],
        arrived, cotangent, row,
        vmem=(True, False, True),
    )[0]
    dots = lax.all_to_all(partial_dots, CTX, 0, 0, tiled=True)
    mixed = call(mixed_kernel, [((rows, width), BF16, False)], arrived, wt, vmem=(True, False))[0]
    partial_router, dlog = call(
        router_kernel,
        [((near, share + far, experts), F32, True), (square, F32, True)],
        dots, routes_t, small, probs, tokens.T, slots,
        vmem=(True, False, True, True, True, True),
    )
    partial_router = lax.all_to_all(partial_router, NEAR, 0, 0, tiled=True)
    mine = call(near_kernel, [((far, share + near, experts), F32, True)], partial_router, vmem=(True,))[0]
    mine = lax.all_to_all(mine, FAR, 0, 0, tiled=True)
    total = call(far_kernel, [((near, share, experts), F32, True)], mine, vmem=(True,))[0]
    router_grad = lax.all_to_all(total, NEAR, 0, 0, tiled=True).reshape(width, experts)
    token_grad = call(
        token_grad_kernel, [((rows, width), BF16, False)], dlog, router_weight, vmem=(True, False)
    )[0]
    slot_grad = owner_rows(everyone, mine, capacity, near, local)
    return (mixed, token_grad, router_grad, slot_grad)


def solution(mesh):
    n = mesh.shape["exp"]
    side = 4 if mesh.shape["ctx"] == 16 else 2
    low = 4 if n == 64 else 2
    split = Mesh(mesh.devices.reshape(side, -1, n // (2 * low), low, 2), CTX + EXP)
    in_specs = (P(EXP, CTX), P(EXP, CTX), P(EXP, None), P(CTX, None), P(EXP, None, CTX))
    out_specs = (P(EXP, CTX), P(EXP, CTX), P(CTX, None), P(EXP, None, CTX))
    return jax.shard_map(step, mesh=split, in_specs=in_specs, out_specs=out_specs, check_vma=False)
```

```python
import functools

import jax
import jax.numpy as jnp
import numpy as np
from jax import lax
from jax.experimental import pallas as pl
from jax.experimental.pallas import tpu as pltpu
from jax.sharding import Mesh
from jax.sharding import PartitionSpec as P


CTX = ("ctx_0", "ctx_1")
EXP = "exp"
NEAR = 8
F32 = jnp.float32
BF16 = jnp.bfloat16
INTERPRET = False
NT = (((1,), (1,)), ((), ()))
HIGHEST = lax.Precision.HIGHEST


def row_order(devices):
    chips = devices // 2
    low, high = NEAR // 2, devices // NEAR
    first = chips // 2 + 2
    return [
        (first + h * low + l) % chips * 2 + core for l in range(low) for h in range(high) for core in range(2)
    ]


def exchange(array, groups):
    return lax.all_to_all(array, EXP, 0, 0, tiled=True, axis_index_groups=groups)


def ring_parts(array, axis):
    size = lax.axis_size(axis)
    parts = [array]
    for shift in range(1, size):
        parts.append(lax.ppermute(array, axis, [(i, (i + shift) % size) for i in range(size)]))
    return parts


def ring_sum(array, axis):
    parts = ring_parts(array, axis)
    total = parts[0]
    for part in parts[1:]:
        total = total + part
    return total


def split3(x):
    hi = x.astype(BF16)
    rest = x - hi.astype(F32)
    mid = rest.astype(BF16)
    lo = (rest - mid.astype(F32)).astype(BF16)
    return hi, mid, lo


def near_memory(array):
    return array if INTERPRET else pltpu.with_memory_space_constraint(array, pltpu.VMEM)


def shaped(shape, dtype, vmem):
    return pltpu.VMEM(shape, dtype) if vmem and not INTERPRET else jax.ShapeDtypeStruct(shape, dtype)


def call(kernel, outs, *args, vmem=None):
    vmem = vmem or (False,) * len(args)
    return pl.pallas_call(
        kernel,
        out_shape=[shaped(*out) for out in outs],
        in_specs=[pl.BlockSpec(memory_space=pltpu.VMEM) for _ in args],
        out_specs=[pl.BlockSpec(memory_space=pltpu.VMEM) for _ in outs],
        interpret=INTERPRET,
    )(*[near_memory(a) if v else a for a, v in zip(args, vmem)])


def pack_kernel(places, perm_ref, in_ref, out_ref):
    local, _, width = in_ref.shape
    dests, each, _ = out_ref.shape
    span = perm_ref.shape[0] // local
    group = span * local // each
    perm = perm_ref[...]
    for c in range(dests // group):
        rows = jnp.concatenate([in_ref[e, c * span : (c + 1) * span, :] for e in range(local)], axis=0)
        out = jnp.dot(perm, rows, preferred_element_type=F32).astype(BF16)
        out = out.reshape(group, each, width)
        for q in range(0, group, 2):
            at = places[c * group + q]
            out_ref[at : at + 2] = out[q : q + 2]


def pack_rows(expert_out, order, capacity, group):
    sources = len(order)
    places = [order.index(s) for s in range(sources)]
    local, _, width = expert_out.shape
    span = group * capacity
    perm = np.zeros((local * span, local * span), np.float32)
    for s in range(group):
        for e in range(local):
            for c in range(capacity):
                perm[(s * local + e) * capacity + c, e * span + s * capacity + c] = 1.0
    return call(
        functools.partial(pack_kernel, places),
        [((sources, local * capacity, width), BF16, True)],
        jnp.asarray(perm, BF16), expert_out,
    )[0]


def gate_kernel(capacity, first, logits_ref, routes_ref, probs_ref, small_ref, row_ref, wt_ref, slots_ref):
    logits = logits_ref[...]
    experts, tokens = logits.shape
    top = routes_ref.shape[0]
    expo = jnp.exp(logits)
    probs = expo / jnp.sum(expo, axis=0, keepdims=True)
    probs_ref[...] = probs
    which = lax.broadcasted_iota(jnp.int32, (experts, tokens), 0)
    hits = [which == routes_ref[k : k + 1, :] for k in range(top)]
    chosen = jnp.concatenate(
        [jnp.sum(jnp.where(hit, probs, 0.0), axis=0, keepdims=True) for hit in hits], axis=0
    )
    total = jnp.sum(chosen, axis=0, keepdims=True)
    gates = chosen / total
    small_ref[0:top, :] = chosen
    small_ref[top : 2 * top, :] = gates
    small_ref[2 * top : 3 * top, :] = jnp.broadcast_to(total, (top, tokens))
    dense = jnp.zeros((experts, tokens), F32)
    member = jnp.zeros((experts, tokens), F32)
    for k in range(top):
        dense = dense + jnp.where(hits[k], gates[k : k + 1, :], 0.0)
        member = member + jnp.where(hits[k], 1.0, 0.0)
    before = lax.broadcasted_iota(jnp.int32, (tokens, tokens), 0)
    after = lax.broadcasted_iota(jnp.int32, (tokens, tokens), 1)
    upper = jnp.where(before < after, 1.0, 0.0).astype(BF16)
    position = jnp.dot(member.astype(BF16), upper, preferred_element_type=F32)
    near, far, _ = slots_ref.shape
    chips = experts // 4
    chip = (which // 4 + chips - first) % chips
    low = near // 2
    order = (chip % low) * (4 * far) + chip // low * 4 + which % 4
    place = order.astype(F32) * float(capacity) + position
    row = jnp.concatenate(
        [jnp.sum(jnp.where(hit, place, 0.0), axis=0, keepdims=True) for hit in hits], axis=0
    )
    row_ref[...] = row
    row_t = row.T
    gates_t = gates.T
    step = min(128, wt_ref.shape[2])
    for c in range(wt_ref.shape[2] // step):
        lane = lax.broadcasted_iota(jnp.int32, (tokens, step), 1).astype(F32) + float(c * step)
        weight = jnp.zeros((tokens, step), F32)
        for k in range(top):
            weight = weight + jnp.where(lane == row_t[:, k : k + 1], gates_t[:, k : k + 1], 0.0)
        for i, term in enumerate(split3(weight)):
            wt_ref[i, :, c * step : (c + 1) * step] = term
    code = jnp.where(member > 0.5, position, -1.0)
    number = after.astype(F32)[0:1, :] + 1.0
    lane = lax.broadcasted_iota(jnp.int32, (experts, 128), 1)
    odd = lax.broadcasted_iota(jnp.int32, (experts, 128), 0) & 1
    lane = lane - 32 * odd
    table = jnp.zeros((experts, 128), F32)
    for s in range(capacity):
        here = code == float(s)
        gate = jnp.sum(jnp.where(here, dense, 0.0), axis=1, keepdims=True)
        token = jnp.sum(jnp.where(here, number, 0.0), axis=1, keepdims=True)
        table = table + jnp.where(lane == s, gate, 0.0) + jnp.where(lane == 16 + s, token, 0.0)
    dest = lax.broadcasted_iota(jnp.int32, (near, far, experts), 1) * near
    dest = dest + lax.broadcasted_iota(jnp.int32, (near, far, experts), 0)
    owner = lax.broadcasted_iota(jnp.int32, (near, far, experts), 2) >> 1
    select = jnp.where(dest == owner, 1.0, 0.0).reshape(near * far, experts).astype(BF16)
    slots = sum(jnp.dot(select, term, preferred_element_type=F32) for term in split3(table))
    slots_ref[...] = slots.reshape(near, far, 128)


def dots_kernel(rows_ref, cot_ref, row_ref, dots_ref):
    sources, each, width = rows_ref.shape
    cot = cot_ref[...]
    top, tokens = row_ref.shape
    group = 8
    span = group * each
    acc = [jnp.zeros((8, tokens), F32) for _ in range(top)]
    index = lax.broadcasted_iota(jnp.int32, (span, tokens), 0).astype(F32)
    for c in range(sources // group):
        rows = rows_ref[c * group : (c + 1) * group].reshape(span, width)
        prod = lax.dot_general(rows, cot, NT, preferred_element_type=F32)
        for k in range(top):
            want = row_ref[k : k + 1, :] - float(c * span)
            part = jnp.where(index == want, prod, 0.0)
            acc[k] = acc[k] + jnp.sum(part.reshape(span // 8, 8, tokens), axis=0)
    dots = jnp.concatenate([jnp.sum(a, axis=0, keepdims=True) for a in acc], axis=0)
    for i in range(dots_ref.shape[0]):
        dots_ref[i] = dots


def mixed_kernel(rows_ref, wt_ref, mixed_ref):
    sources, each, width = rows_ref.shape
    rows = rows_ref[...].reshape(sources * each, width)
    mixed = jnp.dot(wt_ref[0], rows, preferred_element_type=F32)
    for i in range(1, 3):
        mixed = mixed + jnp.dot(wt_ref[i], rows, preferred_element_type=F32)
    mixed_ref[...] = mixed.astype(BF16)


def router_kernel(parts_ref, routes_ref, small_ref, probs_ref, tok_t_ref, slots_ref, part_ref, dlog_ref):
    dots = parts_ref[0]
    for i in range(1, parts_ref.shape[0]):
        dots = dots + parts_ref[i]
    top, _ = dots.shape
    chosen = small_ref[0:top, :]
    gates = small_ref[top : 2 * top, :]
    total = small_ref[2 * top : 3 * top, :]
    dchosen = (dots - jnp.sum(dots * gates, axis=0, keepdims=True)) / total
    level = jnp.sum(chosen * dchosen, axis=0, keepdims=True)
    probs = probs_ref[...]
    which = lax.broadcasted_iota(jnp.int32, probs.shape, 0)
    spread = jnp.zeros(probs.shape, F32)
    for k in range(top):
        spread = spread + jnp.where(which == routes_ref[k : k + 1, :], dchosen[k : k + 1, :], 0.0)
    dlog = probs * (spread - level)
    tok_t = tok_t_ref[...]
    acc = None
    for term in split3(dlog):
        one = lax.dot_general(tok_t, term, NT, preferred_element_type=F32)
        acc = one if acc is None else acc + one
    near, far, _ = slots_ref.shape
    share = acc.shape[0] // near
    for n in range(near):
        part_ref[n, 0:share, :] = acc[n * share : (n + 1) * share, :]
        part_ref[n, share : share + far, :] = slots_ref[n]
    dlog_ref[...] = dlog


def near_kernel(in_ref, out_ref):
    near = in_ref.shape[0]
    far = out_ref.shape[0]
    share = in_ref.shape[1] - far
    total = in_ref[0, 0:share, :]
    for n in range(1, near):
        total = total + in_ref[n, 0:share, :]
    for f in range(far):
        out_ref[f, 0:share, :] = total
        for n in range(near):
            out_ref[f, share + n : share + n + 1, :] = in_ref[n, share + f : share + f + 1, :]


def far_kernel(in_ref, out_ref):
    far = in_ref.shape[0]
    share = out_ref.shape[1]
    total = in_ref[0, 0:share, :]
    for f in range(1, far):
        total = total + in_ref[f, 0:share, :]
    for n in range(out_ref.shape[0]):
        out_ref[n] = total


def token_grad_kernel(dlog_ref, weight_ref, out_ref):
    out_ref[...] = lax.dot_general(
        dlog_ref[...].T, weight_ref[...], NT, precision=HIGHEST, preferred_element_type=F32
    ).astype(BF16)


def owner_kernel(capacity, near, tokens, pair, slots_ref, all_ref, out_ref):
    local = out_ref.shape[0]
    share = slots_ref.shape[1] - near
    group = 4
    rows = group * capacity
    index = lax.broadcasted_iota(jnp.int32, (rows, 128), 0)
    source = sum(jnp.where(index >= q * capacity, 1, 0) for q in range(1, group))
    slot = index - capacity * source
    lane = lax.broadcasted_iota(jnp.int32, (rows, 128), 1)
    column = lax.broadcasted_iota(jnp.int32, (rows, group * tokens), 1).astype(F32)
    base = (source[:, 0:1] * tokens).astype(F32)
    for h in range(pair * near // group):
        step = pl.program_id(0) * pair + h * group // near
        at = share + h * group % near
        table = jnp.broadcast_to(slots_ref[step, at : at + 1, :], (rows, 128))
        for q in range(1, group):
            table = jnp.where(source == q, slots_ref[step, at + q : at + q + 1, :], table)
        gates, picks = [], []
        for e in range(local):
            gates.append(jnp.sum(jnp.where(lane == slot + 32 * e, table, 0.0), axis=1, keepdims=True))
            token = jnp.sum(jnp.where(lane == slot + 32 * e + 16, table, 0.0), axis=1, keepdims=True)
            want = jnp.where(token > 0.5, token - 1.0 + base, -1.0)
            picks.append(jnp.where(column == want, 1.0, 0.0).astype(BF16))
        cot = all_ref[h * group * tokens : (h + 1) * group * tokens, :]
        picked = jnp.dot(jnp.concatenate(picks, axis=0), cot, preferred_element_type=F32)
        for e in range(local):
            out_ref[e, h * rows : (h + 1) * rows, :] = (
                gates[e] * picked[e * rows : (e + 1) * rows, :]
            ).astype(BF16)


def owner_rows(everyone, slots, capacity, near, local):
    far = slots.shape[0]
    count, width = everyone.shape
    tokens = count // (far * near)
    pair = 2
    return pl.pallas_call(
        functools.partial(owner_kernel, capacity, near, tokens, pair),
        grid=(far // pair,),
        in_specs=[
            pl.BlockSpec(memory_space=pltpu.VMEM),
            pl.BlockSpec((pair * near * tokens, width), lambda i: (i, 0)),
        ],
        out_specs=pl.BlockSpec((local, pair * near * capacity, width), lambda i: (0, i, 0)),
        out_shape=jax.ShapeDtypeStruct((local, far * near * capacity, width), BF16),
        interpret=INTERPRET,
    )(near_memory(slots), everyone)


def step(tokens, cotangent, routes, router_weight, expert_out):
    rows, top = routes.shape
    local = expert_out.shape[0]
    sources = lax.axis_size(EXP)
    near = NEAR
    far = sources // near
    order = row_order(sources)
    near_groups = [[f * near + n for n in range(near)] for f in range(far)]
    far_groups = [[f * near + n for f in range(far)] for n in range(near)]
    experts = local * sources
    capacity = expert_out.shape[1] // sources
    width = tokens.shape[1]
    share = width // near
    routes_t = routes.T

    everyone = lax.all_gather(cotangent, EXP, tiled=True)
    sent = pack_rows(expert_out, order, capacity, near)
    arrived = exchange(sent, [order])

    partial_logits = lax.dot_general(
        router_weight, tokens.astype(F32), (((0,), (1,)), ((), ())), precision=HIGHEST
    )
    logits = ring_sum(partial_logits, CTX[1])
    logits = ring_sum(logits, CTX[0])
    square = (experts, rows)
    probs, small, row, wt, slots = call(
        functools.partial(gate_kernel, capacity, order[0] // 2),
        [
            (square, F32, True),
            ((3 * top, rows), F32, True),
            ((top, rows), F32, True),
            ((3, rows, experts * capacity), BF16, False),
            ((near, far, 128), F32, True),
        ],
        logits, routes_t,
    )

    partial_dots = call(
        dots_kernel,
        [((lax.axis_size(CTX), top, rows), F32, True)],
        arrived, cotangent, row,
        vmem=(True, False, True),
    )[0]
    dots = lax.all_to_all(partial_dots, CTX, 0, 0, tiled=True)
    mixed = call(
        mixed_kernel, [((rows, width), BF16, False)], arrived, wt, vmem=(True, False)
    )[0]
    partial_router, dlog = call(
        router_kernel,
        [((near, share + far, experts), F32, True), (square, F32, True)],
        dots, routes_t, small, probs, tokens.T, slots,
        vmem=(True, False, True, True, True, True),
    )
    partial_router = exchange(partial_router, near_groups)
    mine = call(near_kernel, [((far, share + near, experts), F32, True)], partial_router, vmem=(True,))[0]
    mine = exchange(mine, far_groups)
    total = call(far_kernel, [((near, share, experts), F32, True)], mine, vmem=(True,))[0]
    router_grad = exchange(total, near_groups).reshape(width, experts)
    token_grad = call(
        token_grad_kernel, [((rows, width), BF16, False)], dlog, router_weight, vmem=(True, False)
    )[0]
    slot_grad = owner_rows(everyone, mine, capacity, near, local)
    return (mixed, token_grad, router_grad, slot_grad)


def solution(mesh):
    n = mesh.shape["exp"]
    side = 4 if mesh.shape["ctx"] == 16 else 2
    split = Mesh(mesh.devices.reshape(side, -1, n), CTX + (EXP,))
    in_specs = (P(EXP, CTX), P(EXP, CTX), P(EXP, None), P(CTX, None), P(EXP, None, CTX))
    out_specs = (P(EXP, CTX), P(EXP, CTX), P(CTX, None), P(EXP, None, CTX))
    return jax.shard_map(step, mesh=split, in_specs=in_specs, out_specs=out_specs, check_vma=False)
```

```python
import functools

import jax
import jax.numpy as jnp
import numpy as np
from jax import lax
from jax.experimental import pallas as pl
from jax.experimental.pallas import tpu as pltpu
from jax.sharding import Mesh
from jax.sharding import PartitionSpec as P


CTX = ("ctx_0", "ctx_1")
EXP = "exp"
NEAR = 8
F32 = jnp.float32
BF16 = jnp.bfloat16
INTERPRET = False
NT = (((1,), (1,)), ((), ()))
HIGHEST = lax.Precision.HIGHEST


def row_order(devices):
    chips = devices // 2
    low, high = NEAR // 2, devices // NEAR
    first = chips // 2 + 2
    return [
        (first + h * low + l) % chips * 2 + core for l in range(low) for h in range(high) for core in range(2)
    ]


def exchange(array, groups):
    return lax.all_to_all(array, EXP, 0, 0, tiled=True, axis_index_groups=groups)


def ring_parts(array, axis):
    size = lax.axis_size(axis)
    parts = [array]
    for shift in range(1, size):
        parts.append(lax.ppermute(array, axis, [(i, (i + shift) % size) for i in range(size)]))
    return parts


def ring_sum(array, axis):
    parts = ring_parts(array, axis)
    total = parts[0]
    for part in parts[1:]:
        total = total + part
    return total


def split3(x):
    hi = x.astype(BF16)
    rest = x - hi.astype(F32)
    mid = rest.astype(BF16)
    lo = (rest - mid.astype(F32)).astype(BF16)
    return hi, mid, lo


def near_memory(array):
    return array if INTERPRET else pltpu.with_memory_space_constraint(array, pltpu.VMEM)


def shaped(shape, dtype, vmem):
    return pltpu.VMEM(shape, dtype) if vmem and not INTERPRET else jax.ShapeDtypeStruct(shape, dtype)


def call(kernel, outs, *args, vmem=None):
    vmem = vmem or (False,) * len(args)
    return pl.pallas_call(
        kernel,
        out_shape=[shaped(*out) for out in outs],
        in_specs=[pl.BlockSpec(memory_space=pltpu.VMEM) for _ in args],
        out_specs=[pl.BlockSpec(memory_space=pltpu.VMEM) for _ in outs],
        interpret=INTERPRET,
    )(*[near_memory(a) if v else a for a, v in zip(args, vmem)])


def pack_kernel(places, perm_ref, in_ref, out_ref):
    local, _, width = in_ref.shape
    dests, each, _ = out_ref.shape
    span = perm_ref.shape[0] // local
    group = span * local // each
    perm = perm_ref[...]
    for c in range(dests // group):
        rows = jnp.concatenate([in_ref[e, c * span : (c + 1) * span, :] for e in range(local)], axis=0)
        out = jnp.dot(perm, rows, preferred_element_type=F32).astype(BF16)
        out = out.reshape(group, each, width)
        for q in range(0, group, 2):
            at = places[c * group + q]
            out_ref[at : at + 2] = out[q : q + 2]


def pack_rows(expert_out, order, capacity, group):
    sources = len(order)
    places = [order.index(s) for s in range(sources)]
    local, _, width = expert_out.shape
    span = group * capacity
    perm = np.zeros((local * span, local * span), np.float32)
    for s in range(group):
        for e in range(local):
            for c in range(capacity):
                perm[(s * local + e) * capacity + c, e * span + s * capacity + c] = 1.0
    return call(
        functools.partial(pack_kernel, places),
        [((sources, local * capacity, width), BF16, True)],
        jnp.asarray(perm, BF16), expert_out,
    )[0]


def gate_kernel(capacity, first, logits_ref, routes_ref, probs_ref, small_ref, row_ref, wt_ref, slots_ref):
    logits = logits_ref[...]
    experts, tokens = logits.shape
    top = routes_ref.shape[0]
    expo = jnp.exp(logits)
    probs = expo / jnp.sum(expo, axis=0, keepdims=True)
    probs_ref[...] = probs
    which = lax.broadcasted_iota(jnp.int32, (experts, tokens), 0)
    hits = [which == routes_ref[k : k + 1, :] for k in range(top)]
    chosen = jnp.concatenate(
        [jnp.sum(jnp.where(hit, probs, 0.0), axis=0, keepdims=True) for hit in hits], axis=0
    )
    total = jnp.sum(chosen, axis=0, keepdims=True)
    gates = chosen / total
    small_ref[0:top, :] = chosen
    small_ref[top : 2 * top, :] = gates
    small_ref[2 * top : 3 * top, :] = jnp.broadcast_to(total, (top, tokens))
    dense = jnp.zeros((experts, tokens), F32)
    member = jnp.zeros((experts, tokens), F32)
    for k in range(top):
        dense = dense + jnp.where(hits[k], gates[k : k + 1, :], 0.0)
        member = member + jnp.where(hits[k], 1.0, 0.0)
    before = lax.broadcasted_iota(jnp.int32, (tokens, tokens), 0)
    after = lax.broadcasted_iota(jnp.int32, (tokens, tokens), 1)
    upper = jnp.where(before < after, 1.0, 0.0).astype(BF16)
    position = jnp.dot(member.astype(BF16), upper, preferred_element_type=F32)
    near, far, _ = slots_ref.shape
    chips = experts // 4
    chip = (which // 4 + chips - first) % chips
    low = near // 2
    order = (chip % low) * (4 * far) + chip // low * 4 + which % 4
    place = order.astype(F32) * float(capacity) + position
    row = jnp.concatenate(
        [jnp.sum(jnp.where(hit, place, 0.0), axis=0, keepdims=True) for hit in hits], axis=0
    )
    row_ref[...] = row
    row_t = row.T
    gates_t = gates.T
    step = min(128, wt_ref.shape[2])
    for c in range(wt_ref.shape[2] // step):
        lane = lax.broadcasted_iota(jnp.int32, (tokens, step), 1).astype(F32) + float(c * step)
        weight = jnp.zeros((tokens, step), F32)
        for k in range(top):
            weight = weight + jnp.where(lane == row_t[:, k : k + 1], gates_t[:, k : k + 1], 0.0)
        for i, term in enumerate(split3(weight)):
            wt_ref[i, :, c * step : (c + 1) * step] = term
    code = jnp.where(member > 0.5, position, -1.0)
    number = after.astype(F32)[0:1, :] + 1.0
    lane = lax.broadcasted_iota(jnp.int32, (experts, 128), 1)
    odd = lax.broadcasted_iota(jnp.int32, (experts, 128), 0) & 1
    lane = lane - 32 * odd
    table = jnp.zeros((experts, 128), F32)
    for s in range(capacity):
        here = code == float(s)
        gate = jnp.sum(jnp.where(here, dense, 0.0), axis=1, keepdims=True)
        token = jnp.sum(jnp.where(here, number, 0.0), axis=1, keepdims=True)
        table = table + jnp.where(lane == s, gate, 0.0) + jnp.where(lane == 16 + s, token, 0.0)
    dest = lax.broadcasted_iota(jnp.int32, (near, far, experts), 1) * near
    dest = dest + lax.broadcasted_iota(jnp.int32, (near, far, experts), 0)
    owner = lax.broadcasted_iota(jnp.int32, (near, far, experts), 2) >> 1
    select = jnp.where(dest == owner, 1.0, 0.0).reshape(near * far, experts).astype(BF16)
    slots = sum(jnp.dot(select, term, preferred_element_type=F32) for term in split3(table))
    slots_ref[...] = slots.reshape(near, far, 128)


def dots_kernel(rows_ref, cot_ref, row_ref, dots_ref):
    sources, each, width = rows_ref.shape
    cot = cot_ref[...]
    top, tokens = row_ref.shape
    group = 8
    span = group * each
    acc = [jnp.zeros((8, tokens), F32) for _ in range(top)]
    index = lax.broadcasted_iota(jnp.int32, (span, tokens), 0).astype(F32)
    for c in range(sources // group):
        rows = rows_ref[c * group : (c + 1) * group].reshape(span, width)
        prod = lax.dot_general(rows, cot, NT, preferred_element_type=F32)
        for k in range(top):
            want = row_ref[k : k + 1, :] - float(c * span)
            part = jnp.where(index == want, prod, 0.0)
            acc[k] = acc[k] + jnp.sum(part.reshape(span // 8, 8, tokens), axis=0)
    dots = jnp.concatenate([jnp.sum(a, axis=0, keepdims=True) for a in acc], axis=0)
    for i in range(dots_ref.shape[0]):
        dots_ref[i] = dots


def mixed_kernel(rows_ref, wt_ref, mixed_ref):
    sources, each, width = rows_ref.shape
    rows = rows_ref[...].reshape(sources * each, width)
    mixed = jnp.dot(wt_ref[0], rows, preferred_element_type=F32)
    for i in range(1, 3):
        mixed = mixed + jnp.dot(wt_ref[i], rows, preferred_element_type=F32)
    mixed_ref[...] = mixed.astype(BF16)


def router_kernel(parts_ref, routes_ref, small_ref, probs_ref, tok_t_ref, slots_ref, part_ref, dlog_ref):
    dots = parts_ref[0]
    for i in range(1, parts_ref.shape[0]):
        dots = dots + parts_ref[i]
    top, _ = dots.shape
    chosen = small_ref[0:top, :]
    gates = small_ref[top : 2 * top, :]
    total = small_ref[2 * top : 3 * top, :]
    dchosen = (dots - jnp.sum(dots * gates, axis=0, keepdims=True)) / total
    level = jnp.sum(chosen * dchosen, axis=0, keepdims=True)
    probs = probs_ref[...]
    which = lax.broadcasted_iota(jnp.int32, probs.shape, 0)
    spread = jnp.zeros(probs.shape, F32)
    for k in range(top):
        spread = spread + jnp.where(which == routes_ref[k : k + 1, :], dchosen[k : k + 1, :], 0.0)
    dlog = probs * (spread - level)
    tok_t = tok_t_ref[...]
    acc = None
    for term in split3(dlog):
        one = lax.dot_general(tok_t, term, NT, preferred_element_type=F32)
        acc = one if acc is None else acc + one
    near, far, _ = slots_ref.shape
    share = acc.shape[0] // near
    for n in range(near):
        part_ref[n, 0:share, :] = acc[n * share : (n + 1) * share, :]
        part_ref[n, share : share + far, :] = slots_ref[n]
    dlog_ref[...] = dlog


def near_kernel(in_ref, out_ref):
    near = in_ref.shape[0]
    far = out_ref.shape[0]
    share = in_ref.shape[1] - far
    total = in_ref[0, 0:share, :]
    for n in range(1, near):
        total = total + in_ref[n, 0:share, :]
    for f in range(far):
        out_ref[f, 0:share, :] = total
        dest = (f + far // 2) % far
        for n in range(near):
            out_ref[f, share + n : share + n + 1, :] = in_ref[n, share + dest : share + dest + 1, :]


def far_kernel(in_ref, out_ref):
    far = in_ref.shape[0]
    share = out_ref.shape[1]
    total = in_ref[0, 0:share, :]
    for f in range(1, far):
        total = total + in_ref[f, 0:share, :]
    for n in range(out_ref.shape[0]):
        out_ref[n] = total


def token_grad_kernel(dlog_ref, weight_ref, out_ref):
    out_ref[...] = lax.dot_general(
        dlog_ref[...].T, weight_ref[...], NT, precision=HIGHEST, preferred_element_type=F32
    ).astype(BF16)


def owner_kernel(capacity, near, tokens, pair, slots_ref, all_ref, out_ref):
    local = out_ref.shape[0]
    far = slots_ref.shape[0]
    share = slots_ref.shape[1] - near
    group = 4
    rows = group * capacity
    index = lax.broadcasted_iota(jnp.int32, (rows, 128), 0)
    source = sum(jnp.where(index >= q * capacity, 1, 0) for q in range(1, group))
    slot = index - capacity * source
    lane = lax.broadcasted_iota(jnp.int32, (rows, 128), 1)
    column = lax.broadcasted_iota(jnp.int32, (rows, group * tokens), 1).astype(F32)
    base = (source[:, 0:1] * tokens).astype(F32)
    for h in range(pair * near // group):
        step = (pl.program_id(0) * pair + h * group // near + far // 2) % far
        at = share + h * group % near
        table = jnp.broadcast_to(slots_ref[step, at : at + 1, :], (rows, 128))
        for q in range(1, group):
            table = jnp.where(source == q, slots_ref[step, at + q : at + q + 1, :], table)
        gates, picks = [], []
        for e in range(local):
            gates.append(jnp.sum(jnp.where(lane == slot + 32 * e, table, 0.0), axis=1, keepdims=True))
            token = jnp.sum(jnp.where(lane == slot + 32 * e + 16, table, 0.0), axis=1, keepdims=True)
            want = jnp.where(token > 0.5, token - 1.0 + base, -1.0)
            picks.append(jnp.where(column == want, 1.0, 0.0).astype(BF16))
        cot = all_ref[h * group * tokens : (h + 1) * group * tokens, :]
        picked = jnp.dot(jnp.concatenate(picks, axis=0), cot, preferred_element_type=F32)
        for e in range(local):
            out_ref[e, h * rows : (h + 1) * rows, :] = (
                gates[e] * picked[e * rows : (e + 1) * rows, :]
            ).astype(BF16)


def owner_rows(everyone, slots, capacity, near, local):
    far = slots.shape[0]
    count, width = everyone.shape
    tokens = count // (far * near)
    pair = 2
    return pl.pallas_call(
        functools.partial(owner_kernel, capacity, near, tokens, pair),
        grid=(far // pair,),
        in_specs=[
            pl.BlockSpec(memory_space=pltpu.VMEM),
            pl.BlockSpec((pair * near * tokens, width), lambda i: (i, 0)),
        ],
        out_specs=pl.BlockSpec((local, pair * near * capacity, width), lambda i: (0, i, 0)),
        out_shape=jax.ShapeDtypeStruct((local, far * near * capacity, width), BF16),
        interpret=INTERPRET,
    )(near_memory(slots), everyone)


def step(tokens, cotangent, routes, router_weight, expert_out):
    rows, top = routes.shape
    local = expert_out.shape[0]
    sources = lax.axis_size(EXP)
    near = NEAR
    far = sources // near
    order = row_order(sources)
    near_groups = [[f * near + n for n in range(near)] for f in range(far)]
    turn = far // 2
    far_groups = [[(f + turn) % far * near + n for f in range(far)] for n in range(near)]
    experts = local * sources
    capacity = expert_out.shape[1] // sources
    width = tokens.shape[1]
    share = width // near
    routes_t = routes.T

    everyone = lax.all_gather(cotangent, EXP, tiled=True)
    sent = pack_rows(expert_out, order, capacity, near)
    arrived = exchange(sent, [order])

    partial_logits = lax.dot_general(
        router_weight, tokens.astype(F32), (((0,), (1,)), ((), ())), precision=HIGHEST
    )
    logits = ring_sum(partial_logits, CTX[1])
    logits = ring_sum(logits, CTX[0])
    square = (experts, rows)
    probs, small, row, wt, slots = call(
        functools.partial(gate_kernel, capacity, order[0] // 2),
        [
            (square, F32, True),
            ((3 * top, rows), F32, True),
            ((top, rows), F32, True),
            ((3, rows, experts * capacity), BF16, False),
            ((near, far, 128), F32, True),
        ],
        logits, routes_t,
    )

    partial_dots = call(
        dots_kernel,
        [((lax.axis_size(CTX), top, rows), F32, True)],
        arrived, cotangent, row,
        vmem=(True, False, True),
    )[0]
    dots = lax.all_to_all(partial_dots, CTX, 0, 0, tiled=True)
    mixed = call(
        mixed_kernel, [((rows, width), BF16, False)], arrived, wt, vmem=(True, False)
    )[0]
    partial_router, dlog = call(
        router_kernel,
        [((near, share + far, experts), F32, True), (square, F32, True)],
        dots, routes_t, small, probs, tokens.T, slots,
        vmem=(True, False, True, True, True, True),
    )
    partial_router = exchange(partial_router, near_groups)
    mine = call(near_kernel, [((far, share + near, experts), F32, True)], partial_router, vmem=(True,))[0]
    mine = exchange(mine, far_groups)
    total = call(far_kernel, [((near, share, experts), F32, True)], mine, vmem=(True,))[0]
    router_grad = exchange(total, near_groups).reshape(width, experts)
    token_grad = call(
        token_grad_kernel, [((rows, width), BF16, False)], dlog, router_weight, vmem=(True, False)
    )[0]
    slot_grad = owner_rows(everyone, mine, capacity, near, local)
    return (mixed, token_grad, router_grad, slot_grad)


def solution(mesh):
    n = mesh.shape["exp"]
    side = 4 if mesh.shape["ctx"] == 16 else 2
    split = Mesh(mesh.devices.reshape(side, -1, n), CTX + (EXP,))
    in_specs = (P(EXP, CTX), P(EXP, CTX), P(EXP, None), P(CTX, None), P(EXP, None, CTX))
    out_specs = (P(EXP, CTX), P(EXP, CTX), P(CTX, None), P(EXP, None, CTX))
    return jax.shard_map(step, mesh=split, in_specs=in_specs, out_specs=out_specs, check_vma=False)
```

```python
import functools

import jax
import jax.numpy as jnp
import numpy as np
from jax import lax
from jax.experimental import pallas as pl
from jax.experimental.pallas import tpu as pltpu
from jax.sharding import Mesh
from jax.sharding import PartitionSpec as P


CTX = ("ctx_0", "ctx_1")
EXP = "exp"
NEAR = 8
F32 = jnp.float32
BF16 = jnp.bfloat16
INTERPRET = False
NT = (((1,), (1,)), ((), ()))
HIGHEST = lax.Precision.HIGHEST


def row_order(devices):
    chips = devices // 2
    low, high = NEAR // 2, devices // NEAR
    first = chips // 2 + 2
    return [
        (first + h * low + l) % chips * 2 + core for l in range(low) for h in range(high) for core in range(2)
    ]


def near_member(place):
    return (place + NEAR // 2 + 1) % NEAR


def exchange(array, groups):
    return lax.all_to_all(array, EXP, 0, 0, tiled=True, axis_index_groups=groups)


def ring_parts(array, axis):
    size = lax.axis_size(axis)
    parts = [array]
    for shift in range(1, size):
        parts.append(lax.ppermute(array, axis, [(i, (i + shift) % size) for i in range(size)]))
    return parts


def ring_sum(array, axis):
    parts = ring_parts(array, axis)
    total = parts[0]
    for part in parts[1:]:
        total = total + part
    return total


def split3(x):
    hi = x.astype(BF16)
    rest = x - hi.astype(F32)
    mid = rest.astype(BF16)
    lo = (rest - mid.astype(F32)).astype(BF16)
    return hi, mid, lo


def near_memory(array):
    return array if INTERPRET else pltpu.with_memory_space_constraint(array, pltpu.VMEM)


def shaped(shape, dtype, vmem):
    return pltpu.VMEM(shape, dtype) if vmem and not INTERPRET else jax.ShapeDtypeStruct(shape, dtype)


def call(kernel, outs, *args, vmem=None):
    vmem = vmem or (False,) * len(args)
    return pl.pallas_call(
        kernel,
        out_shape=[shaped(*out) for out in outs],
        in_specs=[pl.BlockSpec(memory_space=pltpu.VMEM) for _ in args],
        out_specs=[pl.BlockSpec(memory_space=pltpu.VMEM) for _ in outs],
        interpret=INTERPRET,
    )(*[near_memory(a) if v else a for a, v in zip(args, vmem)])


def pack_kernel(places, perm_ref, in_ref, out_ref):
    local, _, width = in_ref.shape
    dests, each, _ = out_ref.shape
    span = perm_ref.shape[0] // local
    group = span * local // each
    perm = perm_ref[...]
    for c in range(dests // group):
        rows = jnp.concatenate([in_ref[e, c * span : (c + 1) * span, :] for e in range(local)], axis=0)
        out = jnp.dot(perm, rows, preferred_element_type=F32).astype(BF16)
        out = out.reshape(group, each, width)
        for q in range(0, group, 2):
            at = places[c * group + q]
            out_ref[at : at + 2] = out[q : q + 2]


def pack_rows(expert_out, order, capacity, group):
    sources = len(order)
    places = [order.index(s) for s in range(sources)]
    local, _, width = expert_out.shape
    span = group * capacity
    perm = np.zeros((local * span, local * span), np.float32)
    for s in range(group):
        for e in range(local):
            for c in range(capacity):
                perm[(s * local + e) * capacity + c, e * span + s * capacity + c] = 1.0
    return call(
        functools.partial(pack_kernel, places),
        [((sources, local * capacity, width), BF16, True)],
        jnp.asarray(perm, BF16), expert_out,
    )[0]


def gate_kernel(capacity, first, logits_ref, routes_ref, probs_ref, small_ref, row_ref, wt_ref, slots_ref):
    logits = logits_ref[...]
    experts, tokens = logits.shape
    top = routes_ref.shape[0]
    expo = jnp.exp(logits)
    probs = expo / jnp.sum(expo, axis=0, keepdims=True)
    probs_ref[...] = probs
    which = lax.broadcasted_iota(jnp.int32, (experts, tokens), 0)
    hits = [which == routes_ref[k : k + 1, :] for k in range(top)]
    chosen = jnp.concatenate(
        [jnp.sum(jnp.where(hit, probs, 0.0), axis=0, keepdims=True) for hit in hits], axis=0
    )
    total = jnp.sum(chosen, axis=0, keepdims=True)
    gates = chosen / total
    small_ref[0:top, :] = chosen
    small_ref[top : 2 * top, :] = gates
    small_ref[2 * top : 3 * top, :] = jnp.broadcast_to(total, (top, tokens))
    dense = jnp.zeros((experts, tokens), F32)
    member = jnp.zeros((experts, tokens), F32)
    for k in range(top):
        dense = dense + jnp.where(hits[k], gates[k : k + 1, :], 0.0)
        member = member + jnp.where(hits[k], 1.0, 0.0)
    before = lax.broadcasted_iota(jnp.int32, (tokens, tokens), 0)
    after = lax.broadcasted_iota(jnp.int32, (tokens, tokens), 1)
    upper = jnp.where(before < after, 1.0, 0.0).astype(BF16)
    position = jnp.dot(member.astype(BF16), upper, preferred_element_type=F32)
    near, far, _ = slots_ref.shape
    chips = experts // 4
    chip = (which // 4 + chips - first) % chips
    low = near // 2
    order = (chip % low) * (4 * far) + chip // low * 4 + which % 4
    place = order.astype(F32) * float(capacity) + position
    row = jnp.concatenate(
        [jnp.sum(jnp.where(hit, place, 0.0), axis=0, keepdims=True) for hit in hits], axis=0
    )
    row_ref[...] = row
    row_t = row.T
    gates_t = gates.T
    step = min(128, wt_ref.shape[2])
    for c in range(wt_ref.shape[2] // step):
        lane = lax.broadcasted_iota(jnp.int32, (tokens, step), 1).astype(F32) + float(c * step)
        weight = jnp.zeros((tokens, step), F32)
        for k in range(top):
            weight = weight + jnp.where(lane == row_t[:, k : k + 1], gates_t[:, k : k + 1], 0.0)
        for i, term in enumerate(split3(weight)):
            wt_ref[i, :, c * step : (c + 1) * step] = term
    code = jnp.where(member > 0.5, position, -1.0)
    number = after.astype(F32)[0:1, :] + 1.0
    lane = lax.broadcasted_iota(jnp.int32, (experts, 128), 1)
    odd = lax.broadcasted_iota(jnp.int32, (experts, 128), 0) & 1
    lane = lane - 32 * odd
    table = jnp.zeros((experts, 128), F32)
    for s in range(capacity):
        here = code == float(s)
        gate = jnp.sum(jnp.where(here, dense, 0.0), axis=1, keepdims=True)
        token = jnp.sum(jnp.where(here, number, 0.0), axis=1, keepdims=True)
        table = table + jnp.where(lane == s, gate, 0.0) + jnp.where(lane == 16 + s, token, 0.0)
    dest = lax.broadcasted_iota(jnp.int32, (near, far, experts), 1) * near
    dest = dest + near_member(lax.broadcasted_iota(jnp.int32, (near, far, experts), 0))
    owner = lax.broadcasted_iota(jnp.int32, (near, far, experts), 2) >> 1
    select = jnp.where(dest == owner, 1.0, 0.0).reshape(near * far, experts).astype(BF16)
    slots = sum(jnp.dot(select, term, preferred_element_type=F32) for term in split3(table))
    slots_ref[...] = slots.reshape(near, far, 128)


def dots_kernel(rows_ref, cot_ref, row_ref, dots_ref):
    sources, each, width = rows_ref.shape
    cot = cot_ref[...]
    top, tokens = row_ref.shape
    group = 8
    span = group * each
    acc = [jnp.zeros((8, tokens), F32) for _ in range(top)]
    index = lax.broadcasted_iota(jnp.int32, (span, tokens), 0).astype(F32)
    for c in range(sources // group):
        rows = rows_ref[c * group : (c + 1) * group].reshape(span, width)
        prod = lax.dot_general(rows, cot, NT, preferred_element_type=F32)
        for k in range(top):
            want = row_ref[k : k + 1, :] - float(c * span)
            part = jnp.where(index == want, prod, 0.0)
            acc[k] = acc[k] + jnp.sum(part.reshape(span // 8, 8, tokens), axis=0)
    dots = jnp.concatenate([jnp.sum(a, axis=0, keepdims=True) for a in acc], axis=0)
    for i in range(dots_ref.shape[0]):
        dots_ref[i] = dots


def mixed_kernel(rows_ref, wt_ref, mixed_ref):
    sources, each, width = rows_ref.shape
    rows = rows_ref[...].reshape(sources * each, width)
    mixed = jnp.dot(wt_ref[0], rows, preferred_element_type=F32)
    for i in range(1, 3):
        mixed = mixed + jnp.dot(wt_ref[i], rows, preferred_element_type=F32)
    mixed_ref[...] = mixed.astype(BF16)


def router_kernel(parts_ref, routes_ref, small_ref, probs_ref, tok_t_ref, slots_ref, part_ref, dlog_ref):
    dots = parts_ref[0]
    for i in range(1, parts_ref.shape[0]):
        dots = dots + parts_ref[i]
    top, _ = dots.shape
    chosen = small_ref[0:top, :]
    gates = small_ref[top : 2 * top, :]
    total = small_ref[2 * top : 3 * top, :]
    dchosen = (dots - jnp.sum(dots * gates, axis=0, keepdims=True)) / total
    level = jnp.sum(chosen * dchosen, axis=0, keepdims=True)
    probs = probs_ref[...]
    which = lax.broadcasted_iota(jnp.int32, probs.shape, 0)
    spread = jnp.zeros(probs.shape, F32)
    for k in range(top):
        spread = spread + jnp.where(which == routes_ref[k : k + 1, :], dchosen[k : k + 1, :], 0.0)
    dlog = probs * (spread - level)
    tok_t = tok_t_ref[...]
    acc = None
    for term in split3(dlog):
        one = lax.dot_general(tok_t, term, NT, preferred_element_type=F32)
        acc = one if acc is None else acc + one
    near, far, _ = slots_ref.shape
    share = acc.shape[0] // near
    for n in range(near):
        part_ref[n, 0:share, :] = acc[n * share : (n + 1) * share, :]
        part_ref[n, share : share + far, :] = slots_ref[n]
    dlog_ref[...] = dlog


def near_kernel(in_ref, out_ref):
    near = in_ref.shape[0]
    far = out_ref.shape[0]
    share = in_ref.shape[1] - far
    total = in_ref[0, 0:share, :]
    for n in range(1, near):
        total = total + in_ref[n, 0:share, :]
    for f in range(far):
        out_ref[f, 0:share, :] = total
        dest = (f + far // 2) % far
        for n in range(near):
            out_ref[f, share + n : share + n + 1, :] = in_ref[n, share + dest : share + dest + 1, :]


def far_kernel(in_ref, out_ref):
    far = in_ref.shape[0]
    share = out_ref.shape[1]
    total = in_ref[0, 0:share, :]
    for f in range(1, far):
        total = total + in_ref[f, 0:share, :]
    for n in range(out_ref.shape[0]):
        out_ref[n] = total


def token_grad_kernel(dlog_ref, weight_ref, out_ref):
    out_ref[...] = lax.dot_general(
        dlog_ref[...].T, weight_ref[...], NT, precision=HIGHEST, preferred_element_type=F32
    ).astype(BF16)


def owner_kernel(capacity, near, tokens, pair, slots_ref, all_ref, out_ref):
    local = out_ref.shape[0]
    far = slots_ref.shape[0]
    share = slots_ref.shape[1] - near
    members = [near_member(q) for q in range(near)]
    group = 4
    rows = group * capacity
    index = lax.broadcasted_iota(jnp.int32, (rows, 128), 0)
    source = sum(jnp.where(index >= q * capacity, 1, 0) for q in range(1, group))
    slot = index - capacity * source
    lane = lax.broadcasted_iota(jnp.int32, (rows, 128), 1)
    column = lax.broadcasted_iota(jnp.int32, (rows, group * tokens), 1).astype(F32)
    base = (source[:, 0:1] * tokens).astype(F32)
    for h in range(pair * near // group):
        step = (pl.program_id(0) * pair + h * group // near + far // 2) % far
        table = jnp.zeros((rows, 128), F32)
        for q in range(group):
            at = share + members.index(h * group % near + q)
            table = jnp.where(source == q, slots_ref[step, at : at + 1, :], table)
        gates, picks = [], []
        for e in range(local):
            gates.append(jnp.sum(jnp.where(lane == slot + 32 * e, table, 0.0), axis=1, keepdims=True))
            token = jnp.sum(jnp.where(lane == slot + 32 * e + 16, table, 0.0), axis=1, keepdims=True)
            want = jnp.where(token > 0.5, token - 1.0 + base, -1.0)
            picks.append(jnp.where(column == want, 1.0, 0.0).astype(BF16))
        cot = all_ref[h * group * tokens : (h + 1) * group * tokens, :]
        picked = jnp.dot(jnp.concatenate(picks, axis=0), cot, preferred_element_type=F32)
        for e in range(local):
            out_ref[e, h * rows : (h + 1) * rows, :] = (
                gates[e] * picked[e * rows : (e + 1) * rows, :]
            ).astype(BF16)


def owner_rows(everyone, slots, capacity, near, local):
    far = slots.shape[0]
    count, width = everyone.shape
    tokens = count // (far * near)
    pair = 4
    return pl.pallas_call(
        functools.partial(owner_kernel, capacity, near, tokens, pair),
        grid=(far // pair,),
        in_specs=[
            pl.BlockSpec(memory_space=pltpu.VMEM),
            pl.BlockSpec((pair * near * tokens, width), lambda i: (i, 0)),
        ],
        out_specs=pl.BlockSpec((local, pair * near * capacity, width), lambda i: (0, i, 0)),
        out_shape=jax.ShapeDtypeStruct((local, far * near * capacity, width), BF16),
        interpret=INTERPRET,
    )(near_memory(slots), everyone)


def step(tokens, cotangent, routes, router_weight, expert_out):
    rows, top = routes.shape
    local = expert_out.shape[0]
    sources = lax.axis_size(EXP)
    near = NEAR
    far = sources // near
    order = row_order(sources)
    near_groups = [[f * near + near_member(q) for q in range(near)] for f in range(far)]
    turn = far // 2
    far_groups = [[(f + turn) % far * near + n for f in range(far)] for n in range(near)]
    experts = local * sources
    capacity = expert_out.shape[1] // sources
    width = tokens.shape[1]
    share = width // near
    routes_t = routes.T

    everyone = lax.all_gather(cotangent, EXP, tiled=True)
    sent = pack_rows(expert_out, order, capacity, near)
    arrived = exchange(sent, [order])

    partial_logits = lax.dot_general(
        router_weight, tokens.astype(F32), (((0,), (1,)), ((), ())), precision=HIGHEST
    )
    logits = ring_sum(partial_logits, CTX[1])
    logits = ring_sum(logits, CTX[0])
    square = (experts, rows)
    probs, small, row, wt, slots = call(
        functools.partial(gate_kernel, capacity, order[0] // 2),
        [
            (square, F32, True),
            ((3 * top, rows), F32, True),
            ((top, rows), F32, True),
            ((3, rows, experts * capacity), BF16, False),
            ((near, far, 128), F32, True),
        ],
        logits, routes_t,
    )

    partial_dots = call(
        dots_kernel,
        [((lax.axis_size(CTX), top, rows), F32, True)],
        arrived, cotangent, row,
        vmem=(True, False, True),
    )[0]
    dots = lax.all_to_all(partial_dots, CTX, 0, 0, tiled=True)
    mixed = call(
        mixed_kernel, [((rows, width), BF16, False)], arrived, wt, vmem=(True, False)
    )[0]
    partial_router, dlog = call(
        router_kernel,
        [((near, share + far, experts), F32, True), (square, F32, True)],
        dots, routes_t, small, probs, tokens.T, slots,
        vmem=(True, False, True, True, True, True),
    )
    partial_router = exchange(partial_router, near_groups)
    mine = call(near_kernel, [((far, share + near, experts), F32, True)], partial_router, vmem=(True,))[0]
    mine = exchange(mine, far_groups)
    total = call(far_kernel, [((near, share, experts), F32, True)], mine, vmem=(True,))[0]
    router_grad = exchange(total, near_groups).reshape(width, experts)
    token_grad = call(
        token_grad_kernel, [((rows, width), BF16, False)], dlog, router_weight, vmem=(True, False)
    )[0]
    slot_grad = owner_rows(everyone, mine, capacity, near, local)
    return (mixed, token_grad, router_grad, slot_grad)


def solution(mesh):
    n = mesh.shape["exp"]
    side = 4 if mesh.shape["ctx"] == 16 else 2
    split = Mesh(mesh.devices.reshape(side, -1, n), CTX + (EXP,))
    in_specs = (P(EXP, CTX), P(EXP, CTX), P(EXP, None), P(CTX, None), P(EXP, None, CTX))
    out_specs = (P(EXP, CTX), P(EXP, CTX), P(CTX, None), P(EXP, None, CTX))
    return jax.shard_map(step, mesh=split, in_specs=in_specs, out_specs=out_specs, check_vma=False)
```
